128 devices in a mesh: rows: 32 (over y, x_hi, z), cols: 4 (over x_lo, core).
Axes of the slice: x: 4 (x_hi: 2, x_lo: 2; x = x_hi * 2 + x_lo), y: 4, z: 4, core: 2. Of those that a mesh axis runs over, the one named last changes fastest.
Arguments:
- tracks: float32 [1024, 2, 65536], P(('rows', 'cols')), may hold values from -200 to 200
- pixel_order: int32 [65536], P('rows'), may hold values from 0 to 65535, as said below
- pairing: int32 [2, 4], replicated, may hold values from 0 to 2
Outputs:
- rotated: float32 [65536, 2048], P('rows', 'cols')
The draws below stay inside these ranges and needn't reach their ends.
Inputs may be any that keep to these rules, and one draw needn't show every extreme that they name: `pixel_order`: A permutation of 0 to 65535 that maps each aligned block of 2048 rows onto the same block of pixels.
All inputs are finite; a program needn't handle non-finite values.
Results may differ from the reference program's by a relative error of at most 0.0001.
Values sent between devices are 32-bit elements; how exact they have to be, the bound alone decides.
A program may use at most 64 MiB of HBM per device.

```python
import math
import jax
import jax.numpy as jnp
from jax import lax

FRAMES = 1024
NBLK = 16
BLK = 128
M_DEV = 2048
PIXELS = 65536
STEPS = 2
NS_STEPS = 6
N_COLS = 4


def draw_tracks(key, part):
    keys = jax.random.split(key, 5)
    rise = 3.0 ** (jnp.arange(PIXELS, dtype=jnp.float32) / PIXELS - 0.5)
    row_scale = rise * jnp.exp(jax.random.uniform(keys[0], (PIXELS,), jnp.float32, math.log(0.5), math.log(2.0)))
    noise = jnp.clip(jax.random.normal(keys[1], (FRAMES, 2, PIXELS), jnp.float32), -5.0, 5.0)
    common = jax.random.uniform(keys[2], (FRAMES, 2, 1), jnp.float32, -0.5, 0.5)
    column_scale = jnp.exp(jax.random.uniform(keys[3], (FRAMES, 2, 1), jnp.float32, math.log(0.3), math.log(3.0)))
    factor = jnp.clip(jax.random.normal(keys[4], (PIXELS,), jnp.float32), -5.0, 5.0)
    return column_scale * row_scale[None, None, :] * (noise + common * factor[None, None, :])


def draw_pixel_order(key, part):
    block_keys = jax.random.split(key, PIXELS // M_DEV)
    shuffled = jax.vmap(lambda single: jax.random.permutation(single, M_DEV))(block_keys)
    offsets = (jnp.arange(PIXELS // M_DEV, dtype=jnp.int32) * M_DEV)[:, None]
    return (shuffled.astype(jnp.int32) + offsets).reshape(PIXELS)


def with_ends(drawn, rng, smallest, largest):
    longest = drawn.shape.index(max(drawn.shape))
    spots = []
    for shift in (0, 1):
        where = [jax.random.randint(jax.random.fold_in(rng, axis), (), 0, length) for axis, length in enumerate(drawn.shape)]
        where[longest] = (where[longest] + shift) % drawn.shape[longest]
        spots.append(tuple(where))
    return drawn.at[spots[0]].set(smallest).at[spots[1]].set(largest)


def setup_inputs(seed: int = 0) -> dict:
    splits = jax.random.split(jax.random.key(seed), 4)
    tracks = draw_tracks(jax.random.fold_in(splits[3], 71), 0)
    pixel_order = draw_pixel_order(jax.random.fold_in(splits[3], 71), 0)
    pairing = with_ends(jax.random.randint(splits[2], (STEPS, N_COLS), 0, 3), jax.random.fold_in(splits[2], 1), 0, 2).astype(jnp.int32)
    return {"tracks": tracks, "pixel_order": pixel_order, "pairing": pairing}


PAIRINGS = ((0, 1, 2, 3), (0, 2, 1, 3), (0, 3, 1, 2))
UNDOING = ((0, 1, 2, 3), (0, 2, 1, 3), (0, 2, 3, 1))

def rotation(gram_matrix):
    half = gram_matrix.shape[0] // 2
    diagonal = jnp.diagonal(gram_matrix)
    coupling = gram_matrix[:half, half:] / (diagonal[:half, None] + diagonal[None, half:])
    zeros_block = jnp.zeros((half, half), jnp.float32)
    skew_part = jnp.block([[zeros_block, coupling], [-coupling.T, zeros_block]])
    identity = jnp.eye(2 * half, dtype=jnp.float32)
    iterate = (identity + skew_part) / jnp.sqrt(1.0 + jnp.sum(coupling * coupling))
    for count in range(NS_STEPS):
        product = jnp.dot(iterate.T, iterate, precision=lax.Precision.HIGHEST)
        iterate = 1.5 * iterate - 0.5 * jnp.dot(iterate, product, precision=lax.Precision.HIGHEST)
    return iterate

def reference(tracks, pixel_order, pairing):
    residues = NBLK // 2
    shaped = tracks.reshape(BLK, residues, 2, PIXELS)
    matrix = jnp.transpose(shaped, (3, 2, 1, 0)).reshape(PIXELS, NBLK, BLK)
    matrix = jnp.take(matrix, pixel_order.astype(jnp.int32), axis=0)
    table = jnp.array(PAIRINGS, jnp.int32)
    undo_table = jnp.array(UNDOING, jnp.int32)
    for step_index in range(STEPS):
        groups_out = []
        for column_group in range(N_COLS):
            chosen = pairing[step_index, column_group]
            block_set = matrix[:, 4 * column_group:4 * column_group + 4]
            paired = jnp.take(block_set, table[chosen], axis=1).reshape(PIXELS, 2, 2 * BLK)
            turned_pairs = []
            for pair_index in range(2):
                columns = paired[:, pair_index]
                gram_matrix = jnp.dot(columns.T, columns, precision=lax.Precision.HIGHEST)
                turned_pairs.append(jnp.dot(columns, rotation(gram_matrix), precision=lax.Precision.HIGHEST))
            turned = jnp.stack(turned_pairs, axis=1).reshape(PIXELS, 4, BLK)
            groups_out.append(jnp.take(turned, undo_table[chosen], axis=1))
        matrix = jnp.concatenate(groups_out, axis=1)
        if step_index + 1 < STEPS:
            matrix = matrix.at[:, 3::4].set(jnp.roll(matrix[:, 3::4], 1, axis=1))
    matrix = matrix.at[:, 3::4].set(jnp.roll(matrix[:, 3::4], -(STEPS - 1), axis=1))
    return matrix.reshape(PIXELS, NBLK * BLK)
```

```python
import jax, jax.numpy as jnp
from jax import lax
from jax.sharding import PartitionSpec as P
from jax.experimental import pallas as pl
from jax.experimental.pallas import tpu as pltpu
MESH = pl.DeviceIdType.MESH

ORDER = 0

def peer(i, yr, yc):
    if ORDER == 0:
        dc = i % 2; dx = (i // 2) % 4; dz = (i // 8) % 4; dy = i // 32
    elif ORDER == 1:
        dc = i // 64; dx = i % 4; dz = (i // 4) % 4; dy = (i // 16) % 4
    elif ORDER == 2:
        dc = i % 2
        k = i // 2
        a = k % 4; b = (k // 4) % 4; e = k // 16
        dx = a; dy = (a + b) % 4; dz = (a + e + 2*b) % 4
    y = yr // 8; xh = (yr // 4) % 2; z = yr % 4
    xl = yc // 2; core = yc % 2
    x = (xh * 2 + xl + dx) % 4
    yy = (y + dy) % 4; zz = (z + dz) % 4; cc = (core + dc) % 2
    return (yy * 2 + x // 2) * 4 + zz, (x % 2) * 2 + cc

def kernel(v_ref, perm_ref, x_ref, vv, send, recv, xt, tmp, lsem, osem, ssem, rsem):
    yr = lax.axis_index("rows"); yc = lax.axis_index("cols")
    me = yr * 4 + yc
    bar = pltpu.get_barrier_semaphore()
    ld = pltpu.make_async_copy(v_ref, vv, lsem)
    ld.start()
    def sig(i, _):
        r, c = peer(i, yr, yc)
        pl.semaphore_signal(bar, inc=1, device_id=(r, c), device_id_type=MESH)
        return 0
    lax.fori_loop(1, 128, sig, 0)
    ld.wait()
    def dei(i, _):
        f = i // 32; R = i % 32
        for comp in range(2):
            send[f, comp, R] = vv[pl.ds(f * 1024 + R * 32 + comp, 16, stride=2), :]
        return 0
    lax.fori_loop(0, 256, dei, 0, unroll=4)
    pl.semaphore_wait(bar, 127)
    for s in range(4):
        def snd(i, _, s=s):
            r, c = peer(i, yr, yc)
            pltpu.make_async_remote_copy(
                src_ref=send.at[(c % 2) * 4 + s, c // 2, r], dst_ref=recv.at[s, me],
                send_sem=ssem, recv_sem=rsem.at[s], device_id=(r, c), device_id_type=MESH).start()
            return 0
        lax.fori_loop(1, 128, snd, 0)
        recv[s, me] = send[(yc % 2) * 4 + s, yc // 2, yr]
    for s in range(4):
        pltpu.make_async_copy(recv.at[s, pl.ds(0, 127)], recv.at[s, pl.ds(0, 127)], rsem.at[s]).wait()
        for q in range(16):
            blk = recv[s, :, q, :]
            tmp[pl.ds(q * 128, 128), :] = blk.T
        def perm(i, _, s=s):
            for u in range(8):
                k = i * 8 + u
                xt[s, pl.ds(k, 1), :] = tmp[pl.ds(perm_ref[k], 1), :]
            return 0
        lax.fori_loop(0, 256, perm, 0)
        pltpu.make_async_copy(xt.at[s], x_ref.at[s], osem.at[s]).start()
    for s in range(4):
        pltpu.make_async_copy(xt.at[s], x_ref.at[s], osem.at[s]).wait()
        pltpu.make_async_copy(recv.at[s, pl.ds(0, 127)], recv.at[s, pl.ds(0, 127)], ssem).wait()

def exchange(tracks, local):
    v = tracks.reshape(8, 2, 512, 128).transpose(0, 2, 1, 3).reshape(8192, 128)
    f = jnp.float32
    return pl.pallas_call(
        kernel,
        out_shape=jax.ShapeDtypeStruct((4, 2048, 128), f),
        in_specs=[pl.BlockSpec(memory_space=pl.ANY), pl.BlockSpec(memory_space=pltpu.SMEM)],
        out_specs=pl.BlockSpec(memory_space=pl.ANY),
        scratch_shapes=[
            pltpu.VMEM((8192, 128), f), pltpu.VMEM((8, 2, 32, 16, 128), f),
            pltpu.VMEM((4, 128, 16, 128), f), pltpu.VMEM((4, 2048, 128), f), pltpu.VMEM((2048, 128), f),
            pltpu.SemaphoreType.DMA, pltpu.SemaphoreType.DMA((4,)), pltpu.SemaphoreType.DMA, pltpu.SemaphoreType.DMA((4,))],
        compiler_params=pltpu.CompilerParams(collective_id=0, has_side_effects=True, vmem_limit_bytes=40 * 2**20),
    )(v, local)

STEPS = 2
NS_STEPS = 6


PAIRINGS = ((0, 1, 2, 3), (0, 2, 1, 3), (0, 3, 1, 2))
UNDOING = ((0, 1, 2, 3), (0, 2, 1, 3), (0, 2, 3, 1))


def in_blocks(array, dim, size):
    dims = array.shape
    blocks = array.reshape(*dims[:dim], size, dims[dim] // size, *dims[dim + 1 :])
    return jnp.moveaxis(blocks, dim, 0)


def sum_at_owner(array, axis, dim):
    blocks = in_blocks(array, dim, lax.axis_size(axis))
    arrived = lax.all_to_all(blocks, axis, split_axis=0, concat_axis=0, tiled=True)
    return arrived.sum(axis=0)


def rows_for(lines, size):
    spare = -lines.shape[0] % size
    if not spare:
        return lines
    return jnp.concatenate([lines, jnp.zeros((spare, *lines.shape[1:]), lines.dtype)])


def laid_out(blocks, dim):
    blocks = jnp.moveaxis(blocks, 0, dim)
    dims = blocks.shape
    return blocks.reshape(*dims[:dim], dims[dim] * dims[dim + 1], *dims[dim + 2 :])


def from_everyone(array, axis):
    size = lax.axis_size(axis)
    return lax.all_to_all(
        jnp.broadcast_to(array[None], (size, *array.shape)), axis, 0, 0, tiled=True
    )


def gathered_copies(array, axis, dim):
    return laid_out(from_everyone(array, axis), dim)


def nested_sum(array, axes):
    lines = array.reshape(-1, array.shape[-1])
    own = sum_at_owner(rows_for(lines, lax.axis_size(axes)), axes, 0)
    whole = gathered_copies(own, axes, 0)
    return whole[: len(lines)].reshape(array.shape)


def from_behind(value, axis, steps):
    count = lax.axis_size(axis)
    pairs = [(source, (source + steps) % count) for source in range(count)]
    return lax.ppermute(value, axis, pairs)


def rotation(gram_matrix):
    half = gram_matrix.shape[0] // 2
    diagonal = jnp.diagonal(gram_matrix)
    coupling = gram_matrix[:half, half:] / (diagonal[:half, None] + diagonal[None, half:])
    zeros_block = jnp.zeros((half, half), jnp.float32)
    skew_part = jnp.block([[zeros_block, coupling], [-coupling.T, zeros_block]])
    identity = jnp.eye(2 * half, dtype=jnp.float32)
    iterate = (identity + skew_part) / jnp.sqrt(1.0 + jnp.sum(coupling * coupling))
    for count in range(NS_STEPS):
        product = jnp.dot(iterate.T, iterate, precision=lax.Precision.HIGHEST)
        iterate = 1.5 * iterate - 0.5 * jnp.dot(iterate, product, precision=lax.Precision.HIGHEST)
    return iterate


def body(tracks, pixel_order, pairing):
    frames_dev = tracks.shape[0]
    pixel_total = tracks.shape[2]
    row_devices = lax.axis_size("rows")
    row_count = pixel_total // row_devices
    block_width = 128
    local_rows = pixel_order - lax.axis_index("rows") * row_count
    blocks = jnp.transpose(exchange(tracks, local_rows), (1, 0, 2))
    position = lax.axis_index("cols")
    table = jnp.array(PAIRINGS, jnp.int32)
    undo_table = jnp.array(UNDOING, jnp.int32)
    for step_index in range(STEPS):
        chosen = pairing[step_index][position]
        paired = jnp.take(blocks, table[chosen], axis=1).reshape(row_count, 2, 2 * block_width)
        partial_grams = jnp.einsum("mpi,mpj->pij", paired, paired, precision=lax.Precision.HIGHEST)
        gram_sums = nested_sum(partial_grams, "rows")
        rotations = jnp.stack([rotation(gram_sums[0]), rotation(gram_sums[1])])
        turned = jnp.einsum("mpi,pij->mpj", paired, rotations, precision=lax.Precision.HIGHEST)
        blocks = jnp.take(turned.reshape(row_count, 4, block_width), undo_table[chosen], axis=1)
        if step_index + 1 < STEPS:
            shifted = from_behind(blocks[:, 3], "cols", 1)
            blocks = jnp.concatenate([blocks[:, :3], shifted[:, None]], axis=1)
    returned = from_behind(blocks[:, 3], "cols", -(STEPS - 1))
    blocks = jnp.concatenate([blocks[:, :3], returned[:, None]], axis=1)
    return blocks.reshape(row_count, 4 * block_width)


def solution(mesh):
    placed = (P(("rows", "cols"), None, None), P("rows"), P())
    return jax.shard_map(
        body, mesh=mesh, in_specs=placed, out_specs=P("rows", "cols"), check_vma=False
    )
```

```python
import jax
import jax.numpy as jnp
from jax import lax
from jax.experimental import pallas as pl
from jax.experimental.pallas import tpu as pltpu
from jax.sharding import PartitionSpec as P

F32 = jnp.float32
MESH = pl.DeviceIdType.MESH
ANY = pl.BlockSpec(memory_space=pl.ANY)
SMEM = pl.BlockSpec(memory_space=pltpu.SMEM)
HIGH = lax.Precision.HIGH
NS_STEPS = 6
ROWS = 32
COLS = 4
ALL = ROWS * COLS
PIX = 2048
TILE = 256


def product(a, b):
    return jnp.dot(a, b, precision=HIGH, preferred_element_type=F32)


def product_of_rows(a, b):
    return lax.dot_general(a, b, (((0,), (0,)), ((), ())), precision=HIGH, preferred_element_type=F32)


def shifted(yr, yc, dy, dx, dz, dc):
    y = (yr // 8 + dy) % 4
    x = ((yr // 4 % 2) * 2 + yc // 2 + dx) % 4
    z = (yr % 4 + dz) % 4
    return (y * 2 + x // 2) * 4 + z, (x % 2) * 2 + (yc % 2 + dc) % 2


def any_peer(i, yr, yc):
    first, second, third = i // 2 % 4, i // 8 % 4, i // 32
    return shifted(yr, yc, first + second, first, first + third + 2 * second, i % 2)


def row_peer(i, yr):
    y = (yr // 8 + i // 4 % 4) % 4
    x = (yr // 4 % 2 + i // 16) % 2
    z = (yr % 4 + i % 4) % 4
    return (y * 2 + x) * 4 + z


def roles(choice):
    low = jnp.where(choice == 2, 1, 0)
    high = jnp.where(choice == 0, 1, 2)
    return low, high, 2 - choice


def tile(i):
    return pl.ds(pl.multiple_of(i * TILE, TILE), TILE)


def rotations(couplings, state):
    size = 128
    row = lax.broadcasted_iota(jnp.int32, (size, size), 0)
    col = lax.broadcasted_iota(jnp.int32, (size, size), 1)
    eye = jnp.where(row == col, 1.0, 0.0).astype(F32)
    count = 2 * len(couplings)
    flipped = [c.T for c in couplings]
    for k, c in enumerate(couplings):
        total = 1.0 + jnp.sum(jnp.sum(c * c, axis=1, keepdims=True), axis=0, keepdims=True)
        start = eye * (1.0 / jnp.sqrt(total))
        for m, square in ((2 * k, product(c, flipped[k])), (2 * k + 1, product(flipped[k], c))):
            state[m, :size, :] = (eye + square) / total
            state[m, size:, :] = start

    def step(_, carry):
        held = [state[m] for m in range(count)]
        factors = [1.5 * eye - 0.5 * h[:size] for h in held]
        once = [product(h, f) for h, f in zip(held, factors)]
        twice = [product(o[:size], f) for o, f in zip(once, factors)]
        for m in range(count):
            state[m, :size, :] = twice[m]
            state[m, size:, :] = once[m][size:]
        return carry

    lax.fori_loop(0, NS_STEPS - 1, step, 0)
    last = [product(state[m, size:, :], 1.5 * eye - 0.5 * state[m, :size, :]) for m in range(count)]
    out = []
    for k, c in enumerate(couplings):
        cross = product(last[2 * k], c)
        out.append((last[2 * k], cross, -cross.T, last[2 * k + 1]))
    return out


def steps_kernel(
    v_ref, order_ref, pairing_ref, y_ref, z_ref, qn_ref, turn_ref,
    vv, send, recv, flat, xt, yy, z, q, diag, parts, arrived, own, coup, coupn, rot, state,
    load_sem, out_sem, a2a_send, a2a_recv, rs_send, rs_recv, ag_send, ag_recv, z_send, z_recv, q_send, q_recv,
):
    yr, yc = lax.axis_index("rows"), lax.axis_index("cols")
    me = yr * COLS + yc
    after, before = (yc + 1) % COLS, (yc + COLS - 1) % COLS
    barrier = pltpu.get_barrier_semaphore()

    def load(frame):
        lines = pl.ds(frame * 1024, 1024)
        return pltpu.make_async_copy(v_ref.at[lines], vv.at[lines], load_sem.at[frame])

    for s in range(4):
        load(s).start()
        load(4 + s).start()

    def greet(i, carry):
        pl.semaphore_signal(barrier, inc=1, device_id=any_peer(i, yr, yc), device_id_type=MESH)
        return carry

    lax.fori_loop(1, ALL, greet, 0)
    for s in range(4):
        load(s).wait()
        load(4 + s).wait()

        def split(block, carry, s=s):
            for frame in (s, 4 + s):
                for part in range(2):
                    send[frame, part, block] = vv[pl.ds(frame * 1024 + block * 32 + part, 16, stride=2), :]
            return carry

        lax.fori_loop(0, ROWS, split, 0, unroll=2)
        if s == 0:
            pl.semaphore_wait(barrier, ALL - 1)

        def scatter(i, carry, s=s):
            r, c = any_peer(i, yr, yc)
            pltpu.make_async_remote_copy(
                src_ref=send.at[(c % 2) * 4 + s, c // 2, r], dst_ref=recv.at[s, me],
                send_sem=a2a_send, recv_sem=a2a_recv.at[s],
                device_id=(r, c), device_id_type=MESH,
            ).start()
            return carry

        lax.fori_loop(1, ALL, scatter, 0)
        recv[s, me] = send[(yc % 2) * 4 + s, yc // 2, yr]

    def gram(left, right, size):
        def add(i, carry):
            return carry + product_of_rows(left(i), right(i))

        return lax.fori_loop(0, size, add, jnp.zeros((128, 128), F32))

    def squares(block, size):
        def add(i, carry):
            x = block(i)
            return carry + jnp.sum(x * x, axis=0, keepdims=True)

        return lax.fori_loop(0, size, add, jnp.zeros((1, 128), F32))

    tiles = PIX // TILE
    a, b, c = roles(pairing_ref[0, yc])
    gram_p = None
    for s in range(4):
        if s == 3:
            gram_p = gram(lambda i: xt[a, tile(i), :], lambda i: xt[b, tile(i), :], tiles)
        whole = recv.at[s, pl.ds(0, ALL - 1)]
        pltpu.make_async_copy(whole, whole, a2a_recv.at[s]).wait()
        for g in range(16):
            flat[pl.ds(g * 128, 128), :] = recv[s, :, g, :].T

        def place(i, carry, s=s):
            for u in range(8):
                k = i * 8 + u
                xt[s, pl.ds(k, 1), :] = flat[pl.ds(order_ref[k] % PIX, 1), :]
            return carry

        lax.fori_loop(0, PIX // 8, place, 0)
        diag[pl.ds(s, 1), :] = squares(lambda i, s=s: xt[s, tile(i), :], tiles)

    gram_q = gram(lambda i: xt[c, tile(i), :], lambda i: xt[3, tile(i), :], tiles)

    def summed(t, first, second, diagonals):
        for r in range(16):
            parts[t, r, 0:8, :] = first[8 * r : 8 * r + 8]
            parts[t, 16 + r, 0:8, :] = second[8 * r : 8 * r + 8]
        for r in range(ROWS):
            for k in range(4):
                parts[t, r, 8 + k : 9 + k, :] = diagonals[k]

        def deal(i, carry):
            r = row_peer(i, yr)
            pltpu.make_async_remote_copy(
                src_ref=parts.at[t, r], dst_ref=arrived.at[t, yr],
                send_sem=rs_send.at[t], recv_sem=rs_recv.at[t],
                device_id=(r, yc), device_id_type=MESH,
            ).start()
            return carry

        lax.fori_loop(1, ROWS, deal, 0)
        arrived[t, yr] = parts[t, yr]
        whole = arrived.at[t, pl.ds(0, ROWS - 1)]
        pltpu.make_async_copy(whole, whole, rs_recv.at[t]).wait()
        total = arrived[t, 0]
        for r in range(1, ROWS):
            total = total + arrived[t, r]
        second_pair = yr >= 16
        left = jnp.where(second_pair, total[10:11], total[8:9])
        right = jnp.where(second_pair, total[11:12], total[9:10])
        spot = lax.broadcasted_iota(jnp.int32, (8, 128), 0) + 8 * (yr % 16)
        lane = lax.broadcasted_iota(jnp.int32, (8, 128), 1)
        left = jnp.sum(jnp.where(spot == lane, jnp.broadcast_to(left, (8, 128)), 0.0), axis=1, keepdims=True)
        mine = total[0:8] / (left + right)
        own[t] = mine
        coup[t, yr] = mine

        def share(i, carry):
            pltpu.make_async_remote_copy(
                src_ref=own.at[t], dst_ref=coup.at[t, yr],
                send_sem=ag_send.at[t], recv_sem=ag_recv.at[t],
                device_id=(row_peer(i, yr), yc), device_id_type=MESH,
            ).start()
            return carry

        lax.fori_loop(1, ROWS, share, 0)
        if t == 1:
            @pl.when(second_pair)
            def _():
                def lend(i, carry):
                    pltpu.make_async_remote_copy(
                        src_ref=own.at[t], dst_ref=coupn.at[yr - 16],
                        send_sem=ag_send.at[2], recv_sem=ag_recv.at[2],
                        device_id=(row_peer(i, yr), before), device_id_type=MESH,
                    ).start()
                    return carry

                lax.fori_loop(0, ROWS, lend, 0)

        whole = coup.at[t, pl.ds(0, ROWS - 1)]
        pltpu.make_async_copy(whole, whole, ag_recv.at[t]).wait()
        both = coup[t].reshape(256, 128)
        return both[:128], both[128:]

    first, second = summed(
        0, gram_p, gram_q,
        (diag[pl.ds(a, 1), :], diag[pl.ds(b, 1), :], diag[pl.ds(c, 1), :], diag[3:4, :]),
    )
    for k, (top, cross, down, low) in enumerate(rotations((first, second), state)):
        rot[k, :128, :128] = top
        rot[k, :128, 128:] = cross
        rot[k, 128:, :128] = down
        rot[k, 128:, 128:] = low

    def forward(i):
        return pltpu.make_async_remote_copy(
            src_ref=yy.at[3, tile(i)], dst_ref=z.at[tile(i)],
            send_sem=z_send.at[i], recv_sem=z_recv.at[i],
            device_id=(yr, after), device_id_type=MESH,
        )

    def turn_second(i, carry):
        x = jnp.concatenate([xt[c, tile(i), :], xt[3, tile(i), :]], axis=1)
        turned = product(x, rot[1])
        yy[3, tile(i), :] = turned[:, 128:]
        yy[2, tile(i), :] = turned[:, :128]
        forward(i).start()
        return carry

    lax.fori_loop(0, tiles, turn_second, 0)

    def turn_first(i, carry):
        x = jnp.concatenate([xt[a, tile(i), :], xt[b, tile(i), :]], axis=1)
        turned = product(x, rot[0])
        yy[0, tile(i), :] = turned[:, :128]
        yy[1, tile(i), :] = turned[:, 128:]
        return carry

    lax.fori_loop(0, tiles, turn_first, 0)
    keep = pltpu.make_async_copy(yy, y_ref, out_sem.at[0])
    keep.start()

    def role_of(slot):
        return jnp.where(slot == a, 0, jnp.where(slot == b, 1, 2))

    a2, b2, c2 = (role_of(slot) for slot in roles(pairing_ref[1, yc]))
    gram_p = gram(lambda i: yy[a2, tile(i), :], lambda i: yy[b2, tile(i), :], tiles)
    lows = [squares(lambda i, k=k: yy[k, tile(i), :], tiles) for k in (a2, b2, c2)]

    def stage(i, carry):
        q[tile(i), :] = yy[c2, tile(i), :]
        return carry

    lax.fori_loop(0, tiles, stage, 0)

    def meet(i, carry):
        total, square = carry
        forward(i).wait_recv()
        block = z[tile(i), :]
        return (
            total + product_of_rows(q[tile(i), :], block),
            square + jnp.sum(block * block, axis=0, keepdims=True),
        )

    gram_q, last = lax.fori_loop(
        0, tiles, meet, (jnp.zeros((128, 128), F32), jnp.zeros((1, 128), F32))
    )
    back = pltpu.make_async_remote_copy(
        src_ref=q, dst_ref=qn_ref, send_sem=q_send, recv_sem=q_recv,
        device_id=(yr, before), device_id_type=MESH,
    )
    back.start()
    keep_z = pltpu.make_async_copy(z, z_ref, out_sem.at[1])
    keep_z.start()
    first, second = summed(1, gram_p, gram_q, (*lows, last))
    pltpu.make_async_copy(coupn, coupn, ag_recv.at[2]).wait()
    third = coupn[...].reshape(128, 128)
    turns = rotations((first, second, third), state)
    turn_ref[:128, 0:128] = turns[0][0]
    turn_ref[:128, 128:256] = turns[0][1]
    turn_ref[128:, 0:128] = turns[0][2]
    turn_ref[128:, 128:256] = turns[0][3]
    turn_ref[:128, 256:384] = turns[1][0]
    turn_ref[128:, 256:384] = turns[1][2]
    turn_ref[:128, 384:512] = turns[2][1]
    turn_ref[128:, 384:512] = turns[2][3]

    keep.wait()
    keep_z.wait()
    back.wait()

    def drain(i, carry):
        forward(i).wait_send()
        return carry

    lax.fori_loop(0, tiles, drain, 0)
    for s in range(4):
        whole = recv.at[s, pl.ds(0, ALL - 1)]
        pltpu.make_async_copy(whole, whole, a2a_send).wait()
    for t in range(2):
        whole = arrived.at[t, pl.ds(0, ROWS - 1)]
        pltpu.make_async_copy(whole, whole, rs_send.at[t]).wait()
        whole = coup.at[t, pl.ds(0, ROWS - 1)]
        pltpu.make_async_copy(whole, whole, ag_send.at[t]).wait()

    @pl.when(yr >= 16)
    def _():
        whole = coup.at[1]
        pltpu.make_async_copy(whole, whole, ag_send.at[2]).wait()


def two_steps(v, order, pairing):
    tiles = PIX // TILE
    dma = pltpu.SemaphoreType.DMA
    return pl.pallas_call(
        steps_kernel,
        out_shape=(
            jax.ShapeDtypeStruct((4, PIX, 128), F32),
            jax.ShapeDtypeStruct((PIX, 128), F32),
            jax.ShapeDtypeStruct((PIX, 128), F32),
            jax.ShapeDtypeStruct((256, 512), F32),
        ),
        in_specs=[ANY, SMEM, SMEM],
        out_specs=(ANY, ANY, ANY, pl.BlockSpec(memory_space=pltpu.VMEM)),
        scratch_shapes=[
            pltpu.VMEM((8192, 128), F32),
            pltpu.VMEM((8, 2, ROWS, 16, 128), F32),
            pltpu.VMEM((4, ALL, 16, 128), F32),
            pltpu.VMEM((PIX, 128), F32),
            pltpu.VMEM((4, PIX, 128), F32),
            pltpu.VMEM((4, PIX, 128), F32),
            pltpu.VMEM((PIX, 128), F32),
            pltpu.VMEM((PIX, 128), F32),
            pltpu.VMEM((4, 128), F32),
            pltpu.VMEM((2, ROWS, 12, 128), F32),
            pltpu.VMEM((2, ROWS, 12, 128), F32),
            pltpu.VMEM((2, 8, 128), F32),
            pltpu.VMEM((2, ROWS, 8, 128), F32),
            pltpu.VMEM((16, 8, 128), F32),
            pltpu.VMEM((2, 256, 256), F32),
            pltpu.VMEM((6, 256, 128), F32),
            dma((8,)), dma((2,)), dma, dma((4,)), dma((2,)), dma((2,)), dma((3,)), dma((3,)),
            dma((tiles,)), dma((tiles,)), dma, dma,
        ],
        compiler_params=pltpu.CompilerParams(
            collective_id=0, has_side_effects=True, vmem_limit_bytes=48 * 2**20
        ),
    )(v, order, pairing)


def finish_kernel(y_ref, z_ref, qn_ref, turn_ref, pairing_ref, out_ref):
    yc = lax.axis_index("cols")
    a, b, c = roles(pairing_ref[0, yc])
    slots = roles(pairing_ref[1, yc])
    a2, b2, c2 = (jnp.where(slot == a, 0, jnp.where(slot == b, 1, 2)) for slot in slots)
    at = [pl.ds(pl.multiple_of(slot * 128, 128), 128) for slot in slots]
    turned = product(jnp.concatenate([y_ref[a2], y_ref[b2]], axis=1), turn_ref[:, 0:256])
    out_ref[:, at[0]] = turned[:, :128]
    out_ref[:, at[1]] = turned[:, 128:]
    out_ref[:, at[2]] = product(jnp.concatenate([y_ref[c2], z_ref[...]], axis=1), turn_ref[:, 256:384])
    out_ref[:, 384:512] = product(jnp.concatenate([qn_ref[...], y_ref[3]], axis=1), turn_ref[:, 384:512])


def finish(y, z, qn, turn, pairing):
    rows = 512
    return pl.pallas_call(
        finish_kernel,
        grid=(PIX // rows,),
        out_shape=jax.ShapeDtypeStruct((PIX, 512), F32),
        in_specs=[
            pl.BlockSpec((4, rows, 128), lambda i: (0, i, 0)),
            pl.BlockSpec((rows, 128), lambda i: (i, 0)),
            pl.BlockSpec((rows, 128), lambda i: (i, 0)),
            pl.BlockSpec((256, 512), lambda i: (0, 0)),
            SMEM,
        ],
        out_specs=pl.BlockSpec((rows, 512), lambda i: (i, 0)),
        compiler_params=pltpu.CompilerParams(vmem_limit_bytes=24 * 2**20),
    )(y, z, qn, turn, pairing)


def body(tracks, pixel_order, pairing):
    v = tracks.reshape(8, 2, 512, 128).transpose(0, 2, 1, 3).reshape(8192, 128)
    return finish(*two_steps(v, pixel_order, pairing), pairing)


def solution(mesh):
    placed = (P(("rows", "cols"), None, None), P("rows"), P())
    return jax.shard_map(
        body, mesh=mesh, in_specs=placed, out_specs=P("rows", "cols"), check_vma=False
    )
```

```python
import jax
import jax.numpy as jnp
from jax import lax
from jax.experimental import pallas as pl
from jax.experimental.pallas import tpu as pltpu
from jax.sharding import PartitionSpec as P

F32 = jnp.float32
MESH = pl.DeviceIdType.MESH
ANY = pl.BlockSpec(memory_space=pl.ANY)
SMEM = pl.BlockSpec(memory_space=pltpu.SMEM)
INNER = pl.BlockSpec(memory_space=pltpu.VMEM)
HIGH = lax.Precision.HIGH
NS_STEPS = 6
ROWS = 32
COLS = 4
ALL = ROWS * COLS
PIX = 2048
TILE = 512
TILES = PIX // TILE
VMEM = 46 * 2**20


def product(a, b):
    return jnp.dot(a, b, precision=HIGH, preferred_element_type=F32)


def product_of_rows(a, b):
    return lax.dot_general(a, b, (((0,), (0,)), ((), ())), precision=HIGH, preferred_element_type=F32)


def any_peer(i, yr, yc):
    first, second, third = (i >> 1) & 3, (i >> 3) & 3, i >> 5
    y = ((yr >> 3) + first + second) & 3
    x = (((yr >> 1) & 2) + (yc >> 1) + first) & 3
    z = (yr + first + third + 2 * second) & 3
    return (y << 3) + ((x >> 1) << 2) + z, ((x & 1) << 1) + ((yc + i) & 1)


def row_peer(i, yr):
    y = ((yr >> 3) + (i >> 2)) & 3
    x = ((yr >> 2) + (i >> 4)) & 1
    z = (yr + i) & 3
    return (y << 3) + (x << 2) + z


def roles(choice):
    low = jnp.where(choice == 2, 1, 0)
    high = jnp.where(choice == 0, 1, 2)
    return low, high, 2 - choice


def tile(i):
    if isinstance(i, int):
        return pl.ds(i * TILE, TILE)
    return pl.ds(pl.multiple_of(i * TILE, TILE), TILE)


def exact(a, b):
    return jnp.dot(a, b, precision=lax.Precision.HIGHEST, preferred_element_type=F32)


def rotations(couplings, state, weight):
    size = 128
    row = lax.broadcasted_iota(jnp.int32, (size, size), 0)
    col = lax.broadcasted_iota(jnp.int32, (size, size), 1)
    eye = jnp.where(row == col, 1.0, 0.0).astype(F32)
    count = 2 * len(couplings)
    flipped = [c.T for c in couplings]
    for k, c in enumerate(couplings):
        total = 1.0 + jnp.sum(jnp.sum(c * c, axis=1, keepdims=True), axis=0, keepdims=True)
        start = eye * (1.0 / jnp.sqrt(total))
        for m, square in ((2 * k, exact(c, flipped[k])), (2 * k + 1, exact(flipped[k], c))):
            weight[m] = eye + square
            state[m, :size, :] = (eye + square) / total
            state[m, size:, :] = start

    def step(_, carry):
        held = [state[m] for m in range(count)]
        factors = [1.5 * eye - 0.5 * h[:size] for h in held]
        once = [product(h, f) for h, f in zip(held, factors)]
        twice = [product(o[:size], f) for o, f in zip(once, factors)]
        for m in range(count):
            state[m, :size, :] = twice[m]
            state[m, size:, :] = once[m][size:]
        return carry

    lax.fori_loop(0, NS_STEPS - 1, step, 0)
    half = [state[m, size:, :] for m in range(count)]
    met = [exact(weight[m], half[m]) for m in range(count)]
    inner = [exact(half[m], met[m]) for m in range(count)]
    last = [exact(half[m], 1.5 * eye - 0.5 * inner[m]) for m in range(count)]
    out = []
    for k, c in enumerate(couplings):
        cross = exact(last[2 * k], c)
        out.append((last[2 * k], cross, -cross.T, last[2 * k + 1]))
    return out


def steps_kernel(
    v_ref, order_ref, pairing_ref, y_ref, z_ref, qn_ref, turn_ref,
    vv, send, recv, flat, xt, yy, zc, z3, z, q, diag, parts, arrived, own, coup, coupn, rot, state, weight,
    load_sem, out_sem, a2a_send, a2a_recv, rs_send, rs_recv, ag_send, ag_recv, lend_send, lend_recv,
    z_send, z_recv, q_send, q_recv,
):
    yr, yc = lax.axis_index("rows"), lax.axis_index("cols")
    me = yr * COLS + yc
    after, before = (yc + 1) & 3, (yc + 3) & 3
    barrier = pltpu.get_barrier_semaphore()

    def load(frame):
        lines = pl.ds(frame * 1024, 1024)
        return pltpu.make_async_copy(v_ref.at[lines], vv.at[lines], load_sem.at[frame])

    for s in range(4):
        load(s).start()
        load(4 + s).start()

    def greet(i, carry):
        pl.semaphore_signal(barrier, inc=1, device_id=any_peer(i, yr, yc), device_id_type=MESH)
        return carry

    lax.fori_loop(1, ALL, greet, 0, unroll=9)
    for s in range(4):
        load(s).wait()
        load(4 + s).wait()

        def split(block, carry, s=s):
            for frame in (s, 4 + s):
                for part in range(2):
                    send[frame, part, block] = vv[pl.ds(frame * 1024 + block * 32 + part, 16, stride=2), :]
            return carry

        lax.fori_loop(0, ROWS, split, 0, unroll=2)
        if s == 0:
            pl.semaphore_wait(barrier, ALL - 1)

        def scatter(i, carry, s=s):
            r, c = any_peer(i, yr, yc)
            pltpu.make_async_remote_copy(
                src_ref=send.at[((c & 1) << 2) + s, c >> 1, r], dst_ref=recv.at[s, me],
                send_sem=a2a_send, recv_sem=a2a_recv.at[s],
                device_id=(r, c), device_id_type=MESH,
            ).start()
            return carry

        lax.fori_loop(1, ALL, scatter, 0)
        recv[s, me] = send[((yc & 1) << 2) + s, yc >> 1, yr]

    def gram(left, right):
        def add(i, carry):
            return carry + product_of_rows(left(i), right(i))

        return lax.fori_loop(0, TILES, add, jnp.zeros((128, 128), F32))

    def squares(block):
        def add(i, carry):
            x = block(i)
            return carry + jnp.sum(x * x, axis=0, keepdims=True)

        return lax.fori_loop(0, TILES, add, jnp.zeros((1, 128), F32))

    def place(s):
        def move(i, carry):
            for u in range(16):
                k = i * 16 + u
                xt[s, pl.ds(k, 1), :] = flat[s, pl.ds(order_ref[k] & (PIX - 1), 1), :]
            return carry

        lax.fori_loop(0, PIX // 16, move, 0)

    a, b, c = roles(pairing_ref[0, yc])
    gram_p = None
    for s in range(4):
        if s == 3:
            gram_p = gram(lambda i: flat[a, tile(i), :], lambda i: flat[b, tile(i), :])
        whole = recv.at[s, pl.ds(0, ALL - 1)]
        pltpu.make_async_copy(whole, whole, a2a_recv.at[s]).wait()
        for g in range(16):
            flat[s, pl.ds(g * 128, 128), :] = recv[s, :, g, :].T
        diag[pl.ds(s, 1), :] = squares(lambda i, s=s: flat[s, tile(i), :])
        if s < 3:
            place(s)

    def summed(t, first, second, diagonals, early, late):
        low = jnp.concatenate(diagonals, axis=0)
        for r in range(16):
            parts[t, r, 0:8, :] = first[8 * r : 8 * r + 8]
            parts[t, 16 + r, 0:8, :] = second[8 * r : 8 * r + 8]
        for r in range(ROWS):
            parts[t, r, 8:12, :] = low

        def deal(i, carry):
            r = row_peer(i, yr)
            pltpu.make_async_remote_copy(
                src_ref=parts.at[t, r], dst_ref=arrived.at[t, yr],
                send_sem=rs_send.at[t], recv_sem=rs_recv.at[t],
                device_id=(r, yc), device_id_type=MESH,
            ).start()
            return carry

        lax.fori_loop(1, ROWS, deal, 0, unroll=True)
        arrived[t, yr] = parts[t, yr]
        early()
        whole = arrived.at[t, pl.ds(0, ROWS - 1)]
        pltpu.make_async_copy(whole, whole, rs_recv.at[t]).wait()
        total = arrived[t, 0]
        for r in range(1, ROWS):
            total = total + arrived[t, r]
        second_pair = yr >= 16
        left = jnp.where(second_pair, total[10:11], total[8:9])
        right = jnp.where(second_pair, total[11:12], total[9:10])
        spot = lax.broadcasted_iota(jnp.int32, (8, 128), 0) + 8 * (yr & 15)
        lane = lax.broadcasted_iota(jnp.int32, (8, 128), 1)
        left = jnp.sum(jnp.where(spot == lane, jnp.broadcast_to(left, (8, 128)), 0.0), axis=1, keepdims=True)
        mine = total[0:8] / (left + right)
        own[t] = mine
        coup[t, yr] = mine

        def share(i, carry):
            pltpu.make_async_remote_copy(
                src_ref=own.at[t], dst_ref=coup.at[t, yr],
                send_sem=ag_send.at[t], recv_sem=ag_recv.at[t],
                device_id=(row_peer(i, yr), yc), device_id_type=MESH,
            ).start()
            return carry

        lax.fori_loop(1, ROWS, share, 0, unroll=True)

        @pl.when(second_pair)
        def _():
            def lend(i, carry):
                pltpu.make_async_remote_copy(
                    src_ref=own.at[t], dst_ref=coupn.at[t, yr - 16],
                    send_sem=lend_send.at[t], recv_sem=lend_recv.at[t],
                    device_id=(row_peer(i, yr), before if t else after), device_id_type=MESH,
                ).start()
                return carry

            lax.fori_loop(0, ROWS, lend, 0, unroll=True)

        late()
        whole = coup.at[t, pl.ds(0, ROWS - 1)]
        pltpu.make_async_copy(whole, whole, ag_recv.at[t]).wait()
        whole = coupn.at[t]
        pltpu.make_async_copy(whole, whole, lend_recv.at[t]).wait()
        both = coup[t].reshape(256, 128)
        return both[:128], both[128:], coupn[t].reshape(128, 128)

    half = PIX // 2
    upper, lower = pl.ds(0, half), pl.ds(half, half)
    raw = TILES - 1

    def forward(k):
        at = pl.ds(k % raw * TILE, TILE)
        pairs = ((q.at[at], zc.at[at]), (xt.at[3, at], z3.at[at]))
        src, dst = pairs[k // raw] if k < 2 * raw else (yy.at[3, pl.ds(raw * TILE, TILE)], z.at[pl.ds(raw * TILE, TILE)])
        return pltpu.make_async_remote_copy(
            src_ref=src, dst_ref=dst, send_sem=z_send.at[k], recv_sem=z_recv.at[k],
            device_id=(yr, after), device_id_type=MESH,
        )

    q[pl.ds(0, TILE), :] = xt[c, pl.ds(0, TILE), :]
    forward(0).start()
    gram_q = gram(lambda i: flat[c, tile(i), :], lambda i: flat[3, tile(i), :])

    def early_first():
        for k in range(1, raw):
            q[pl.ds(k * TILE, TILE), :] = xt[c, pl.ds(k * TILE, TILE), :]
            forward(k).start()
        place(3)

    def late_first():
        for k in range(raw, 2 * raw):
            forward(k).start()

    first, second, third = summed(
        0, gram_p, gram_q,
        (diag[pl.ds(a, 1), :], diag[pl.ds(b, 1), :], diag[pl.ds(c, 1), :], diag[3:4, :]),
        early_first, late_first,
    )
    for k, (top, cross, down, low) in enumerate(rotations((first, second, third), state, weight)):
        rot[k, :128, :128] = top
        rot[k, :128, 128:] = cross
        rot[k, 128:, :128] = down
        rot[k, 128:, 128:] = low

    def turn_second(i):
        x = jnp.concatenate([xt[c, tile(i), :], xt[3, tile(i), :]], axis=1)
        turned = product(x, rot[1])
        yy[3, tile(i), :] = turned[:, 128:]
        yy[2, tile(i), :] = turned[:, :128]

    def turn_first(i):
        x = jnp.concatenate([xt[a, tile(i), :], xt[b, tile(i), :]], axis=1)
        turned = product(x, rot[0])
        yy[0, tile(i), :] = turned[:, :128]
        yy[1, tile(i), :] = turned[:, 128:]

    def turn_own(i, carry):
        turn_first(i)
        turn_second(i)
        return carry

    turn_second(raw)
    forward(2 * raw).start()
    turn_first(raw)
    lax.fori_loop(0, raw, turn_own, 0)
    keep = pltpu.make_async_copy(yy, y_ref, out_sem.at[0])
    keep.start()

    def role_of(slot):
        return jnp.where(slot == a, 0, jnp.where(slot == b, 1, 2))

    a2, b2, c2 = (role_of(slot) for slot in roles(pairing_ref[1, yc]))
    gram_p = gram(lambda i: yy[a2, tile(i), :], lambda i: yy[b2, tile(i), :])
    lows = [squares(lambda i, k=k: yy[k, tile(i), :]) for k in (a2, b2, c2)]

    for k in range(2 * raw):
        forward(k).wait_recv()

    def meet(i, block, carry):
        total, square = carry
        return (
            total + product_of_rows(yy[c2, tile(i), :], block),
            square + jnp.sum(block * block, axis=0, keepdims=True),
        )

    def turn_and_meet(i, carry):
        x = jnp.concatenate([zc[tile(i), :], z3[tile(i), :]], axis=1)
        block = product(x, rot[2, :, 128:])
        z[tile(i), :] = block
        return meet(i, block, carry)

    met = lax.fori_loop(
        0, raw, turn_and_meet, (jnp.zeros((128, 128), F32), jnp.zeros((1, 128), F32))
    )
    forward(2 * raw).wait_recv()
    gram_q, last = meet(raw, z[tile(raw), :], met)
    keep_z = pltpu.make_async_copy(z, z_ref, out_sem.at[1])
    keep_z.start()
    for k in range(raw):
        forward(k).wait_send()

    def backward(k):
        part = (upper, lower)[k]
        return pltpu.make_async_remote_copy(
            src_ref=q.at[part], dst_ref=qn_ref.at[part], send_sem=q_send.at[k], recv_sem=q_recv.at[k],
            device_id=(yr, before), device_id_type=MESH,
        )

    def early_second():
        q[upper, :] = yy[c2, upper, :]
        backward(0).start()
        q[lower, :] = yy[c2, lower, :]

    first, second, third = summed(
        1, gram_p, gram_q, (*lows, last), early_second, lambda: backward(1).start()
    )
    turns = rotations((first, second, third), state, weight)
    turn_ref[:128, 0:128] = turns[0][0]
    turn_ref[:128, 128:256] = turns[0][1]
    turn_ref[128:, 0:128] = turns[0][2]
    turn_ref[128:, 128:256] = turns[0][3]
    turn_ref[:128, 256:384] = turns[1][0]
    turn_ref[128:, 256:384] = turns[1][2]
    turn_ref[:128, 384:512] = turns[2][1]
    turn_ref[128:, 384:512] = turns[2][3]

    keep.wait()
    keep_z.wait()
    for k in range(raw, 2 * raw + 1):
        forward(k).wait_send()
    for k in range(2):
        backward(k).wait()
    for s in range(4):
        whole = recv.at[s, pl.ds(0, ALL - 1)]
        pltpu.make_async_copy(whole, whole, a2a_send).wait()
    for t in range(2):
        whole = arrived.at[t, pl.ds(0, ROWS - 1)]
        pltpu.make_async_copy(whole, whole, rs_send.at[t]).wait()
        whole = coup.at[t, pl.ds(0, ROWS - 1)]
        pltpu.make_async_copy(whole, whole, ag_send.at[t]).wait()

    @pl.when(yr >= 16)
    def _():
        for t in range(2):
            whole = coup.at[t]
            pltpu.make_async_copy(whole, whole, lend_send.at[t]).wait()


def two_steps(v, order, pairing):
    dma = pltpu.SemaphoreType.DMA
    return pl.pallas_call(
        steps_kernel,
        out_shape=(
            jax.ShapeDtypeStruct((4, PIX, 128), F32),
            jax.ShapeDtypeStruct((PIX, 128), F32),
            jax.ShapeDtypeStruct((PIX, 128), F32),
            jax.ShapeDtypeStruct((256, 512), F32),
        ),
        in_specs=[ANY, SMEM, SMEM],
        out_specs=(ANY, ANY, ANY, pl.BlockSpec(memory_space=pltpu.VMEM)),
        scratch_shapes=[
            pltpu.VMEM((8192, 128), F32),
            pltpu.VMEM((8, 2, ROWS, 16, 128), F32),
            pltpu.VMEM((4, ALL, 16, 128), F32),
            pltpu.VMEM((4, PIX, 128), F32),
            pltpu.VMEM((4, PIX, 128), F32),
            pltpu.VMEM((4, PIX, 128), F32),
            pltpu.VMEM((PIX, 128), F32),
            pltpu.VMEM((PIX, 128), F32),
            pltpu.VMEM((PIX, 128), F32),
            pltpu.VMEM((PIX, 128), F32),
            pltpu.VMEM((4, 128), F32),
            pltpu.VMEM((2, ROWS, 12, 128), F32),
            pltpu.VMEM((2, ROWS, 12, 128), F32),
            pltpu.VMEM((2, 8, 128), F32),
            pltpu.VMEM((2, ROWS, 8, 128), F32),
            pltpu.VMEM((2, 16, 8, 128), F32),
            pltpu.VMEM((3, 256, 256), F32),
            pltpu.VMEM((6, 256, 128), F32),
            pltpu.VMEM((6, 128, 128), F32),
            dma((8,)), dma((2,)), dma, dma((4,)), dma((2,)), dma((2,)), dma((2,)), dma((2,)), dma((2,)), dma((2,)),
            dma((2 * TILES - 1,)), dma((2 * TILES - 1,)), dma((2,)), dma((2,)),
        ],
        compiler_params=pltpu.CompilerParams(
            collective_id=0, has_side_effects=True, vmem_limit_bytes=VMEM
        ),
    )(v, order, pairing)


def finish_kernel(y_ref, z_ref, qn_ref, turn_ref, pairing_ref, out_ref):
    yc = lax.axis_index("cols")
    a, b, c = roles(pairing_ref[0, yc])
    slots = roles(pairing_ref[1, yc])
    a2, b2, c2 = (jnp.where(slot == a, 0, jnp.where(slot == b, 1, 2)) for slot in slots)
    at = [pl.ds(pl.multiple_of(slot * 128, 128), 128) for slot in slots]
    here = tile(pl.program_id(0))

    def turned(first, second, columns):
        return product(jnp.concatenate([first[here, :], second[here, :]], axis=1), turn_ref[:, columns])

    pair = turned(y_ref.at[a2], y_ref.at[b2], pl.ds(0, 256))
    out_ref[:, at[0]] = pair[:, :128]
    out_ref[:, at[1]] = pair[:, 128:]
    out_ref[:, at[2]] = turned(y_ref.at[c2], z_ref, pl.ds(256, 128))
    out_ref[:, 384:512] = turned(qn_ref, y_ref.at[3], pl.ds(384, 128))


def finish(y, z, qn, turn, pairing):
    rows = TILE
    return pl.pallas_call(
        finish_kernel,
        grid=(PIX // rows,),
        out_shape=jax.ShapeDtypeStruct((PIX, 512), F32),
        in_specs=[INNER, INNER, INNER, INNER, SMEM],
        out_specs=pl.BlockSpec((rows, 512), lambda i: (i, 0)),
        compiler_params=pltpu.CompilerParams(vmem_limit_bytes=24 * 2**20),
    )(y, z, qn, turn, pairing)


def body(tracks, pixel_order, pairing):
    v = tracks.reshape(8, 2, 512, 128).transpose(0, 2, 1, 3).reshape(8192, 128)
    return finish(*two_steps(v, pixel_order, pairing), pairing)


def solution(mesh):
    placed = (P(("rows", "cols"), None, None), P("rows"), P())
    return jax.shard_map(
        body, mesh=mesh, in_specs=placed, out_specs=P("rows", "cols"), check_vma=False
    )
```

```python
import jax
import jax.numpy as jnp
from jax import lax
from jax.experimental import pallas as pl
from jax.experimental.pallas import tpu as pltpu
from jax.sharding import PartitionSpec as P

F32 = jnp.float32
MESH = pl.DeviceIdType.MESH
ANY = pl.BlockSpec(memory_space=pl.ANY)
SMEM = pl.BlockSpec(memory_space=pltpu.SMEM)
INNER = pl.BlockSpec(memory_space=pltpu.VMEM)
HIGH = lax.Precision.HIGH
NS_STEPS = 6
ROWS = 32
COLS = 4
ALL = ROWS * COLS
PIX = 2048
TILE = 512
TILES = PIX // TILE
VMEM = 46 * 2**20


def product(a, b):
    return jnp.dot(a, b, precision=HIGH, preferred_element_type=F32)


def product_of_rows(a, b):
    return lax.dot_general(a, b, (((0,), (0,)), ((), ())), precision=HIGH, preferred_element_type=F32)


def any_peer(i, yr, yc):
    first, second, third = (i >> 1) & 3, (i >> 3) & 3, i >> 5
    y = ((yr >> 3) + first + second) & 3
    x = (((yr >> 1) & 2) + (yc >> 1) + first) & 3
    z = (yr + first + third + 2 * second) & 3
    return (y << 3) + ((x >> 1) << 2) + z, ((x & 1) << 1) + ((yc + i) & 1)


def row_peer(i, yr):
    y = ((yr >> 3) + (i >> 2)) & 3
    x = ((yr >> 2) + (i >> 4)) & 1
    z = (yr + i) & 3
    return (y << 3) + (x << 2) + z


def hops(i):
    ring = (0, 1, 2, 1)
    return ring[i & 3] + ring[i >> 2 & 3] + 2 * (i >> 4)


FAR_FIRST = sorted(range(ROWS), key=hops, reverse=True)


def roles(choice):
    low = jnp.where(choice == 2, 1, 0)
    high = jnp.where(choice == 0, 1, 2)
    return low, high, 2 - choice


def tile(i):
    if isinstance(i, int):
        return pl.ds(i * TILE, TILE)
    return pl.ds(pl.multiple_of(i * TILE, TILE), TILE)


def exact(a, b):
    return jnp.dot(a, b, precision=lax.Precision.HIGHEST, preferred_element_type=F32)


def rotations(couplings, state, weight):
    size = 128
    row = lax.broadcasted_iota(jnp.int32, (size, size), 0)
    col = lax.broadcasted_iota(jnp.int32, (size, size), 1)
    eye = jnp.where(row == col, 1.0, 0.0).astype(F32)
    count = 2 * len(couplings)
    flipped = [c.T for c in couplings]
    for k, c in enumerate(couplings):
        total = 1.0 + jnp.sum(jnp.sum(c * c, axis=1, keepdims=True), axis=0, keepdims=True)
        start = eye * (1.0 / jnp.sqrt(total))
        for m, square in ((2 * k, exact(c, flipped[k])), (2 * k + 1, exact(flipped[k], c))):
            weight[m] = eye + square
            state[m, :size, :] = (eye + square) / total
            state[m, size:, :] = start

    def step(_, carry):
        held = [state[m] for m in range(count)]
        factors = [1.5 * eye - 0.5 * h[:size] for h in held]
        once = [product(h, f) for h, f in zip(held, factors)]
        twice = [product(o[:size], f) for o, f in zip(once, factors)]
        for m in range(count):
            state[m, :size, :] = twice[m]
            state[m, size:, :] = once[m][size:]
        return carry

    lax.fori_loop(0, NS_STEPS - 1, step, 0, unroll=True)
    half = [state[m, size:, :] for m in range(count)]
    met = [exact(weight[m], half[m]) for m in range(count)]
    inner = [exact(half[m], met[m]) for m in range(count)]
    crossed = [exact(half[2 * k], c) for k, c in enumerate(couplings)]
    factors = [1.5 * eye - 0.5 * n for n in inner]
    last = [exact(h, f) for h, f in zip(half, factors)]
    out = []
    for k in range(len(couplings)):
        cross = exact(factors[2 * k], crossed[k])
        out.append((last[2 * k], cross, -cross.T, last[2 * k + 1]))
    return out


def steps_kernel(
    v_ref, order_ref, pairing_ref, y_ref, z_ref, qn_ref, turn_ref,
    vv, send, recv, flat, xt, yy, zc, z3, z, q, diag, parts, arrived, own, coup, coupn, rot, state, weight,
    load_sem, out_sem, a2a_send, a2a_recv, rs_send, rs_recv, ag_send, ag_recv, lend_send, lend_recv,
    z_send, z_recv, q_send, q_recv,
):
    yr, yc = lax.axis_index("rows"), lax.axis_index("cols")
    me = yr * COLS + yc
    after, before = (yc + 1) & 3, (yc + 3) & 3
    barrier = pltpu.get_barrier_semaphore()

    def load(frame):
        lines = pl.ds(frame * 1024, 1024)
        return pltpu.make_async_copy(v_ref.at[lines], vv.at[lines], load_sem.at[frame])

    for s in range(4):
        load(s).start()
        load(4 + s).start()

    def greet(i, carry):
        pl.semaphore_signal(barrier, inc=1, device_id=any_peer(i, yr, yc), device_id_type=MESH)
        return carry

    lax.fori_loop(1, ALL, greet, 0, unroll=9)
    for s in range(4):
        load(s).wait()
        load(4 + s).wait()

        def split(block, carry, s=s):
            for frame in (s, 4 + s):
                for part in range(2):
                    send[frame, part, block] = vv[pl.ds(frame * 1024 + block * 32 + part, 16, stride=2), :]
            return carry

        lax.fori_loop(0, ROWS, split, 0, unroll=2)
        if s == 0:
            pl.semaphore_wait(barrier, ALL - 1)

        def scatter(i, carry, s=s):
            r, c = any_peer(i, yr, yc)
            pltpu.make_async_remote_copy(
                src_ref=send.at[((c & 1) << 2) + s, c >> 1, r], dst_ref=recv.at[s, me],
                send_sem=a2a_send, recv_sem=a2a_recv.at[s],
                device_id=(r, c), device_id_type=MESH,
            ).start()
            return carry

        lax.fori_loop(1, ALL, scatter, 0)
        recv[s, me] = send[((yc & 1) << 2) + s, yc >> 1, yr]

    def gram(left, right):
        def add(i, carry):
            return carry + product_of_rows(left(i), right(i))

        return lax.fori_loop(0, TILES, add, jnp.zeros((128, 128), F32))

    def squares(block):
        def add(i, carry):
            x = block(i)
            return carry + jnp.sum(x * x, axis=0, keepdims=True)

        return lax.fori_loop(0, TILES, add, jnp.zeros((1, 128), F32))

    def place(s):
        def move(i, carry):
            for u in range(16):
                k = i * 16 + u
                xt[s, pl.ds(k, 1), :] = flat[s, pl.ds(order_ref[k] & (PIX - 1), 1), :]
            return carry

        lax.fori_loop(0, PIX // 16, move, 0)

    a, b, c = roles(pairing_ref[0, yc])
    gram_p = None
    for s in range(4):
        if s == 3:
            gram_p = gram(lambda i: flat[a, tile(i), :], lambda i: flat[b, tile(i), :])
        whole = recv.at[s, pl.ds(0, ALL - 1)]
        pltpu.make_async_copy(whole, whole, a2a_recv.at[s]).wait()
        for g in range(16):
            flat[s, pl.ds(g * 128, 128), :] = recv[s, :, g, :].T
        diag[pl.ds(s, 1), :] = squares(lambda i, s=s: flat[s, tile(i), :])
        if s < 3:
            place(s)

    def summed(t, first, second, diagonals, early, late):
        lows = [jnp.concatenate(diagonals[k : k + 2], axis=0) for k in (0, 2)]
        for r in range(16):
            parts[t, r, 0:8, :] = first[8 * r : 8 * r + 8]
            parts[t, 16 + r, 0:8, :] = second[8 * r : 8 * r + 8]
        for r in range(ROWS):
            parts[t, r, 8:10, :] = lows[r // 16]

        for i in FAR_FIRST[:-1]:
            r = row_peer(i, yr)
            pltpu.make_async_remote_copy(
                src_ref=parts.at[t, r], dst_ref=arrived.at[t, yr],
                send_sem=rs_send.at[t], recv_sem=rs_recv.at[t],
                device_id=(r, yc), device_id_type=MESH,
            ).start()
        arrived[t, yr] = parts[t, yr]
        early()
        whole = arrived.at[t, pl.ds(0, ROWS - 1)]
        pltpu.make_async_copy(whole, whole, rs_recv.at[t]).wait()
        total = arrived[t, 0]
        for r in range(1, ROWS):
            total = total + arrived[t, r]
        second_pair = yr >= 16
        left, right = total[8:9], total[9:10]
        spot = lax.broadcasted_iota(jnp.int32, (8, 128), 0) + 8 * (yr & 15)
        lane = lax.broadcasted_iota(jnp.int32, (8, 128), 1)
        left = jnp.sum(jnp.where(spot == lane, jnp.broadcast_to(left, (8, 128)), 0.0), axis=1, keepdims=True)
        mine = total[0:8] / (left + right)
        own[t] = mine
        coup[t, yr] = mine

        for i in FAR_FIRST[:-1]:
            pltpu.make_async_remote_copy(
                src_ref=own.at[t], dst_ref=coup.at[t, yr],
                send_sem=ag_send.at[t], recv_sem=ag_recv.at[t],
                device_id=(row_peer(i, yr), yc), device_id_type=MESH,
            ).start()

        @pl.when(second_pair)
        def _():
            for i in FAR_FIRST:
                pltpu.make_async_remote_copy(
                    src_ref=own.at[t], dst_ref=coupn.at[t, yr - 16],
                    send_sem=lend_send.at[t], recv_sem=lend_recv.at[t],
                    device_id=(row_peer(i, yr), before if t else after), device_id_type=MESH,
                ).start()

        late()
        whole = coup.at[t, pl.ds(0, ROWS - 1)]
        pltpu.make_async_copy(whole, whole, ag_recv.at[t]).wait()
        whole = coupn.at[t]
        pltpu.make_async_copy(whole, whole, lend_recv.at[t]).wait()
        both = coup[t].reshape(256, 128)
        return both[:128], both[128:], coupn[t].reshape(128, 128)

    half = PIX // 2
    upper, lower = pl.ds(0, half), pl.ds(half, half)
    raw = TILES - 1

    def forward(k):
        at = pl.ds(k % raw * TILE, TILE)
        pairs = ((q.at[at], zc.at[at]), (xt.at[3, at], z3.at[at]))
        src, dst = pairs[k // raw] if k < 2 * raw else (yy.at[3, pl.ds(raw * TILE, TILE)], z.at[pl.ds(raw * TILE, TILE)])
        return pltpu.make_async_remote_copy(
            src_ref=src, dst_ref=dst, send_sem=z_send.at[k], recv_sem=z_recv.at[k],
            device_id=(yr, after), device_id_type=MESH,
        )

    q[pl.ds(0, TILE), :] = xt[c, pl.ds(0, TILE), :]
    forward(0).start()
    gram_q = gram(lambda i: flat[c, tile(i), :], lambda i: flat[3, tile(i), :])

    def early_first():
        for k in range(1, raw):
            q[pl.ds(k * TILE, TILE), :] = xt[c, pl.ds(k * TILE, TILE), :]
            forward(k).start()
        place(3)

    def late_first():
        for k in range(raw, 2 * raw):
            forward(k).start()

    first, second, third = summed(
        0, gram_p, gram_q,
        (diag[pl.ds(a, 1), :], diag[pl.ds(b, 1), :], diag[pl.ds(c, 1), :], diag[3:4, :]),
        early_first, late_first,
    )
    for k, (top, cross, down, low) in enumerate(rotations((first, second, third), state, weight)):
        rot[k, :128, :128] = top
        rot[k, :128, 128:] = cross
        rot[k, 128:, :128] = down
        rot[k, 128:, 128:] = low

    def turn_second(i):
        x = jnp.concatenate([xt[c, tile(i), :], xt[3, tile(i), :]], axis=1)
        turned = product(x, rot[1])
        yy[3, tile(i), :] = turned[:, 128:]
        yy[2, tile(i), :] = turned[:, :128]

    def turn_first(i):
        x = jnp.concatenate([xt[a, tile(i), :], xt[b, tile(i), :]], axis=1)
        turned = product(x, rot[0])
        yy[0, tile(i), :] = turned[:, :128]
        yy[1, tile(i), :] = turned[:, 128:]

    def turn_own(i, carry):
        turn_first(i)
        turn_second(i)
        return carry

    turn_second(raw)
    forward(2 * raw).start()
    turn_first(raw)
    lax.fori_loop(0, raw, turn_own, 0)
    keep = pltpu.make_async_copy(yy, y_ref, out_sem.at[0])
    keep.start()

    def role_of(slot):
        return jnp.where(slot == a, 0, jnp.where(slot == b, 1, 2))

    a2, b2, c2 = (role_of(slot) for slot in roles(pairing_ref[1, yc]))
    gram_p = gram(lambda i: yy[a2, tile(i), :], lambda i: yy[b2, tile(i), :])
    lows = [squares(lambda i, k=k: yy[k, tile(i), :]) for k in (a2, b2, c2)]

    for k in range(2 * raw):
        forward(k).wait_recv()

    def meet(i, block, carry):
        total, square = carry
        return (
            total + product_of_rows(yy[c2, tile(i), :], block),
            square + jnp.sum(block * block, axis=0, keepdims=True),
        )

    def turn_and_meet(i, carry):
        x = jnp.concatenate([zc[tile(i), :], z3[tile(i), :]], axis=1)
        block = product(x, rot[2, :, 128:])
        z[tile(i), :] = block
        return meet(i, block, carry)

    met = lax.fori_loop(
        0, raw, turn_and_meet, (jnp.zeros((128, 128), F32), jnp.zeros((1, 128), F32))
    )
    forward(2 * raw).wait_recv()
    gram_q, last = meet(raw, z[tile(raw), :], met)
    keep_z = pltpu.make_async_copy(z, z_ref, out_sem.at[1])
    keep_z.start()
    for k in range(raw):
        forward(k).wait_send()

    def backward(k):
        part = (upper, lower)[k]
        return pltpu.make_async_remote_copy(
            src_ref=q.at[part], dst_ref=qn_ref.at[part], send_sem=q_send.at[k], recv_sem=q_recv.at[k],
            device_id=(yr, before), device_id_type=MESH,
        )

    def early_second():
        q[upper, :] = yy[c2, upper, :]
        backward(0).start()
        q[lower, :] = yy[c2, lower, :]

    first, second, third = summed(
        1, gram_p, gram_q, (*lows, last), early_second, lambda: backward(1).start()
    )
    turns = rotations((first, second, third), state, weight)
    turn_ref[:128, 0:128] = turns[0][0]
    turn_ref[:128, 128:256] = turns[0][1]
    turn_ref[128:, 0:128] = turns[0][2]
    turn_ref[128:, 128:256] = turns[0][3]
    turn_ref[:128, 256:384] = turns[1][0]
    turn_ref[128:, 256:384] = turns[1][2]
    turn_ref[:128, 384:512] = turns[2][1]
    turn_ref[128:, 384:512] = turns[2][3]

    keep.wait()
    keep_z.wait()
    for k in range(raw, 2 * raw + 1):
        forward(k).wait_send()
    for k in range(2):
        backward(k).wait()
    for s in range(4):
        whole = recv.at[s, pl.ds(0, ALL - 1)]
        pltpu.make_async_copy(whole, whole, a2a_send).wait()
    for t in range(2):
        whole = arrived.at[t, pl.ds(0, ROWS - 1)]
        pltpu.make_async_copy(whole, whole, rs_send.at[t]).wait()
        whole = coup.at[t, pl.ds(0, ROWS - 1)]
        pltpu.make_async_copy(whole, whole, ag_send.at[t]).wait()

    @pl.when(yr >= 16)
    def _():
        for t in range(2):
            whole = coup.at[t]
            pltpu.make_async_copy(whole, whole, lend_send.at[t]).wait()


def two_steps(v, order, pairing):
    dma = pltpu.SemaphoreType.DMA
    return pl.pallas_call(
        steps_kernel,
        out_shape=(
            jax.ShapeDtypeStruct((4, PIX, 128), F32),
            jax.ShapeDtypeStruct((PIX, 128), F32),
            jax.ShapeDtypeStruct((PIX, 128), F32),
            jax.ShapeDtypeStruct((256, 512), F32),
        ),
        in_specs=[ANY, SMEM, SMEM],
        out_specs=(ANY, ANY, ANY, pl.BlockSpec(memory_space=pltpu.VMEM)),
        scratch_shapes=[
            pltpu.VMEM((8192, 128), F32),
            pltpu.VMEM((8, 2, ROWS, 16, 128), F32),
            pltpu.VMEM((4, ALL, 16, 128), F32),
            pltpu.VMEM((4, PIX, 128), F32),
            pltpu.VMEM((4, PIX, 128), F32),
            pltpu.VMEM((4, PIX, 128), F32),
            pltpu.VMEM((PIX, 128), F32),
            pltpu.VMEM((PIX, 128), F32),
            pltpu.VMEM((PIX, 128), F32),
            pltpu.VMEM((PIX, 128), F32),
            pltpu.VMEM((4, 128), F32),
            pltpu.VMEM((2, ROWS, 10, 128), F32),
            pltpu.VMEM((2, ROWS, 10, 128), F32),
            pltpu.VMEM((2, 8, 128), F32),
            pltpu.VMEM((2, ROWS, 8, 128), F32),
            pltpu.VMEM((2, 16, 8, 128), F32),
            pltpu.VMEM((3, 256, 256), F32),
            pltpu.VMEM((6, 256, 128), F32),
            pltpu.VMEM((6, 128, 128), F32),
            dma((8,)), dma((2,)), dma, dma((4,)), dma((2,)), dma((2,)), dma((2,)), dma((2,)), dma((2,)), dma((2,)),
            dma((2 * TILES - 1,)), dma((2 * TILES - 1,)), dma((2,)), dma((2,)),
        ],
        compiler_params=pltpu.CompilerParams(
            collective_id=0, has_side_effects=True, vmem_limit_bytes=VMEM
        ),
    )(v, order, pairing)


def finish_kernel(y_ref, z_ref, qn_ref, turn_ref, pairing_ref, out_ref):
    yc = lax.axis_index("cols")
    a, b, c = roles(pairing_ref[0, yc])
    slots = roles(pairing_ref[1, yc])
    a2, b2, c2 = (jnp.where(slot == a, 0, jnp.where(slot == b, 1, 2)) for slot in slots)
    at = [pl.ds(pl.multiple_of(slot * 128, 128), 128) for slot in slots]
    here = tile(pl.program_id(0))

    def turned(first, second, columns):
        return product(jnp.concatenate([first[here, :], second[here, :]], axis=1), turn_ref[:, columns])

    pair = turned(y_ref.at[a2], y_ref.at[b2], pl.ds(0, 256))
    out_ref[:, at[0]] = pair[:, :128]
    out_ref[:, at[1]] = pair[:, 128:]
    out_ref[:, at[2]] = turned(y_ref.at[c2], z_ref, pl.ds(256, 128))
    out_ref[:, 384:512] = turned(qn_ref, y_ref.at[3], pl.ds(384, 128))


def finish(y, z, qn, turn, pairing):
    rows = TILE
    return pl.pallas_call(
        finish_kernel,
        grid=(PIX // rows,),
        out_shape=jax.ShapeDtypeStruct((PIX, 512), F32),
        in_specs=[INNER, INNER, INNER, INNER, SMEM],
        out_specs=pl.BlockSpec((rows, 512), lambda i: (i, 0)),
        compiler_params=pltpu.CompilerParams(vmem_limit_bytes=24 * 2**20),
    )(y, z, qn, turn, pairing)


def body(tracks, pixel_order, pairing):
    v = tracks.reshape(8, 2, 512, 128).transpose(0, 2, 1, 3).reshape(8192, 128)
    return finish(*two_steps(v, pixel_order, pairing), pairing)


def solution(mesh):
    placed = (P(("rows", "cols"), None, None), P("rows"), P())
    return jax.shard_map(
        body, mesh=mesh, in_specs=placed, out_specs=P("rows", "cols"), check_vma=False
    )
```

```python
import jax
import jax.numpy as jnp
from jax import lax
from jax.experimental import pallas as pl
from jax.experimental.pallas import tpu as pltpu
from jax.sharding import PartitionSpec as P

F32 = jnp.float32
MESH = pl.DeviceIdType.MESH
ANY = pl.BlockSpec(memory_space=pl.ANY)
SMEM = pl.BlockSpec(memory_space=pltpu.SMEM)
INNER = pl.BlockSpec(memory_space=pltpu.VMEM)
HIGH = lax.Precision.HIGH
NS_STEPS = 6
ROWS = 32
COLS = 4
ALL = ROWS * COLS
PIX = 2048
TILE = 512
TILES = PIX // TILE
VMEM = 46 * 2**20


def product(a, b):
    return jnp.dot(a, b, precision=HIGH, preferred_element_type=F32)


def product_of_rows(a, b):
    return lax.dot_general(a, b, (((0,), (0,)), ((), ())), precision=HIGH, preferred_element_type=F32)


def any_peer(i, yr, yc):
    first, second, third = (i >> 1) & 3, (i >> 3) & 3, i >> 5
    y = ((yr >> 3) + first + second) & 3
    x = (((yr >> 1) & 2) + (yc >> 1) + first) & 3
    z = (yr + first + third + 2 * second) & 3
    return (y << 3) + ((x >> 1) << 2) + z, ((x & 1) << 1) + ((yc + i) & 1)


def row_peer(i, yr):
    y = ((yr >> 3) + (i >> 2)) & 3
    x = ((yr >> 2) + (i >> 4)) & 1
    z = (yr + i) & 3
    return (y << 3) + (x << 2) + z


def hops(i):
    ring = (0, 1, 2, 1)
    return ring[i & 3] + ring[i >> 2 & 3] + 2 * (i >> 4)


FAR_FIRST = sorted(range(ROWS), key=hops, reverse=True)


def roles(choice):
    low = jnp.where(choice == 2, 1, 0)
    high = jnp.where(choice == 0, 1, 2)
    return low, high, 2 - choice


def tile(i):
    if isinstance(i, int):
        return pl.ds(i * TILE, TILE)
    return pl.ds(pl.multiple_of(i * TILE, TILE), TILE)


def exact(a, b):
    return jnp.dot(a, b, precision=lax.Precision.HIGHEST, preferred_element_type=F32)


def rotations(couplings, state, weight):
    size = 128
    row = lax.broadcasted_iota(jnp.int32, (size, size), 0)
    col = lax.broadcasted_iota(jnp.int32, (size, size), 1)
    eye = jnp.where(row == col, 1.0, 0.0).astype(F32)
    count = 2 * len(couplings)
    flipped = [c.T for c in couplings]
    for k, c in enumerate(couplings):
        total = 1.0 + jnp.sum(jnp.sum(c * c, axis=1, keepdims=True), axis=0, keepdims=True)
        start = eye * (1.0 / jnp.sqrt(total))
        for m, square in ((2 * k, exact(c, flipped[k])), (2 * k + 1, exact(flipped[k], c))):
            weight[m] = eye + square
            state[m, :size, :] = (eye + square) / total
            state[m, size:, :] = start

    def step(_, carry):
        held = [state[m] for m in range(count)]
        factors = [1.5 * eye - 0.5 * h[:size] for h in held]
        once = [product(h, f) for h, f in zip(held, factors)]
        twice = [product(o[:size], f) for o, f in zip(once, factors)]
        for m in range(count):
            state[m, :size, :] = twice[m]
            state[m, size:, :] = once[m][size:]
        return carry

    lax.fori_loop(0, NS_STEPS - 1, step, 0, unroll=True)
    half = [state[m, size:, :] for m in range(count)]
    met = [exact(weight[m], half[m]) for m in range(count)]
    inner = [exact(half[m], met[m]) for m in range(count)]
    crossed = [exact(half[2 * k], c) for k, c in enumerate(couplings)]
    factors = [1.5 * eye - 0.5 * n for n in inner]
    last = [exact(h, f) for h, f in zip(half, factors)]
    out = []
    for k in range(len(couplings)):
        cross = exact(factors[2 * k], crossed[k])
        out.append((last[2 * k], cross, -cross.T, last[2 * k + 1]))
    return out


def steps_kernel(
    v_ref, order_ref, pairing_ref, y_ref, z_ref, qn_ref, turn_ref,
    vv, send, recv, flat, xt, yy, zc, z3, z, q, diag, parts, arrived, own, coup, coupn, rot, state, weight,
    load_sem, out_sem, a2a_send, a2a_recv, rs_send, rs_recv, ag_send, ag_recv, lend_send, lend_recv,
    z_send, z_recv, q_send, q_recv,
):
    yr, yc = lax.axis_index("rows"), lax.axis_index("cols")
    me = yr * COLS + yc
    after, before = (yc + 1) & 3, (yc + 3) & 3
    barrier = pltpu.get_barrier_semaphore()

    def load(frame):
        lines = pl.ds(frame * 1024, 1024)
        return pltpu.make_async_copy(v_ref.at[lines], vv.at[lines], load_sem.at[frame])

    for s in range(4):
        load(s).start()
        load(4 + s).start()

    def greet(i, carry):
        pl.semaphore_signal(barrier, inc=1, device_id=any_peer(i, yr, yc), device_id_type=MESH)
        return carry

    lax.fori_loop(1, ALL, greet, 0, unroll=9)
    for s in range(4):
        load(s).wait()
        load(4 + s).wait()

        def split(block, carry, s=s):
            for frame in (s, 4 + s):
                for part in range(2):
                    send[frame, part, block] = vv[pl.ds(frame * 1024 + block * 32 + part, 16, stride=2), :]
            return carry

        lax.fori_loop(0, ROWS, split, 0, unroll=2)
        if s == 0:
            pl.semaphore_wait(barrier, ALL - 1)

        def scatter(i, carry, s=s):
            r, c = any_peer(i, yr, yc)
            pltpu.make_async_remote_copy(
                src_ref=send.at[((c & 1) << 2) + s, c >> 1, r], dst_ref=recv.at[s, me],
                send_sem=a2a_send, recv_sem=a2a_recv.at[s],
                device_id=(r, c), device_id_type=MESH,
            ).start()
            return carry

        lax.fori_loop(1, ALL, scatter, 0)
        recv[s, me] = send[((yc & 1) << 2) + s, yc >> 1, yr]

    def gram(left, right):
        def add(i, carry):
            return carry + product_of_rows(left(i), right(i))

        return lax.fori_loop(0, TILES, add, jnp.zeros((128, 128), F32))

    def squares(block):
        def add(i, carry):
            x = block(i)
            return carry + jnp.sum(x * x, axis=0, keepdims=True)

        return lax.fori_loop(0, TILES, add, jnp.zeros((1, 128), F32))

    def place(s):
        def move(i, carry):
            for u in range(16):
                k = i * 16 + u
                xt[s, pl.ds(k, 1), :] = flat[s, pl.ds(order_ref[k] & (PIX - 1), 1), :]
            return carry

        lax.fori_loop(0, PIX // 16, move, 0)

    a, b, c = roles(pairing_ref[0, yc])
    gram_p = None
    for s in range(4):
        if s == 3:
            gram_p = gram(lambda i: flat[a, tile(i), :], lambda i: flat[b, tile(i), :])
        whole = recv.at[s, pl.ds(0, ALL - 1)]
        pltpu.make_async_copy(whole, whole, a2a_recv.at[s]).wait()
        for g in range(16):
            flat[s, pl.ds(g * 128, 128), :] = recv[s, :, g, :].T
        diag[pl.ds(s, 1), :] = squares(lambda i, s=s: flat[s, tile(i), :])
        if s < 3:
            place(s)

    def summed(t, first, second, diagonals, early, late):
        lows = [jnp.concatenate(diagonals[k : k + 2], axis=0) for k in (0, 2)]
        for r in range(16):
            parts[t, r, 0:8, :] = first[8 * r : 8 * r + 8]
            parts[t, 16 + r, 0:8, :] = second[8 * r : 8 * r + 8]
        for r in range(ROWS):
            parts[t, r, 8:10, :] = lows[r // 16]

        for i in FAR_FIRST[:-1]:
            r = row_peer(i, yr)
            pltpu.make_async_remote_copy(
                src_ref=parts.at[t, r], dst_ref=arrived.at[t, yr],
                send_sem=rs_send.at[t], recv_sem=rs_recv.at[t],
                device_id=(r, yc), device_id_type=MESH,
            ).start()
        arrived[t, yr] = parts[t, yr]
        early()
        whole = arrived.at[t, pl.ds(0, ROWS - 1)]
        pltpu.make_async_copy(whole, whole, rs_recv.at[t]).wait()
        total = arrived[t, 0]
        for r in range(1, ROWS):
            total = total + arrived[t, r]
        second_pair = yr >= 16
        left, right = total[8:9], total[9:10]
        spot = lax.broadcasted_iota(jnp.int32, (8, 128), 0) + 8 * (yr & 15)
        lane = lax.broadcasted_iota(jnp.int32, (8, 128), 1)
        left = jnp.sum(jnp.where(spot == lane, jnp.broadcast_to(left, (8, 128)), 0.0), axis=1, keepdims=True)
        mine = total[0:8] / (left + right)
        own[t] = mine
        coup[t, yr] = mine

        for i in FAR_FIRST[:-1]:
            pltpu.make_async_remote_copy(
                src_ref=own.at[t], dst_ref=coup.at[t, yr],
                send_sem=ag_send.at[t], recv_sem=ag_recv.at[t],
                device_id=(row_peer(i, yr), yc), device_id_type=MESH,
            ).start()

        @pl.when(second_pair)
        def _():
            for i in FAR_FIRST:
                pltpu.make_async_remote_copy(
                    src_ref=own.at[t], dst_ref=coupn.at[t, yr - 16],
                    send_sem=lend_send.at[t], recv_sem=lend_recv.at[t],
                    device_id=(row_peer(i, yr), before if t else after), device_id_type=MESH,
                ).start()

        late()
        whole = coup.at[t, pl.ds(0, ROWS - 1)]
        pltpu.make_async_copy(whole, whole, ag_recv.at[t]).wait()
        whole = coupn.at[t]
        pltpu.make_async_copy(whole, whole, lend_recv.at[t]).wait()
        both = coup[t].reshape(256, 128)
        return both[:128], both[128:], coupn[t].reshape(128, 128)

    half = PIX // 2
    upper, lower = pl.ds(0, half), pl.ds(half, half)
    raw = TILES - 1

    def forward(k):
        at = pl.ds(k % raw * TILE, TILE)
        pairs = ((q.at[at], zc.at[at]), (xt.at[3, at], z3.at[at]))
        src, dst = pairs[k // raw] if k < 2 * raw else (yy.at[3, pl.ds(raw * TILE, TILE)], z.at[pl.ds(raw * TILE, TILE)])
        return pltpu.make_async_remote_copy(
            src_ref=src, dst_ref=dst, send_sem=z_send.at[k], recv_sem=z_recv.at[k],
            device_id=(yr, after), device_id_type=MESH,
        )

    q[pl.ds(0, TILE), :] = xt[c, pl.ds(0, TILE), :]
    forward(0).start()
    gram_q = gram(lambda i: flat[c, tile(i), :], lambda i: flat[3, tile(i), :])

    def early_first():
        for k in range(1, raw):
            q[pl.ds(k * TILE, TILE), :] = xt[c, pl.ds(k * TILE, TILE), :]
            forward(k).start()
        place(3)

    def late_first():
        for k in range(raw, 2 * raw):
            forward(k).start()

    first, second, third = summed(
        0, gram_p, gram_q,
        (diag[pl.ds(a, 1), :], diag[pl.ds(b, 1), :], diag[pl.ds(c, 1), :], diag[3:4, :]),
        early_first, late_first,
    )
    for k, (top, cross, down, low) in enumerate(rotations((first, second, third), state, weight)):
        rot[k, :128, :128] = top
        rot[k, :128, 128:] = cross
        rot[k, 128:, :128] = down
        rot[k, 128:, 128:] = low

    def square(x):
        return jnp.sum(x * x, axis=0, keepdims=True)

    def turn_second(i):
        x = jnp.concatenate([xt[c, tile(i), :], xt[3, tile(i), :]], axis=1)
        turned = product(x, rot[1])
        yy[3, tile(i), :] = turned[:, 128:]
        yy[2, tile(i), :] = turned[:, :128]
        return square(turned[:, :128])

    def turn_first(i):
        x = jnp.concatenate([xt[a, tile(i), :], xt[b, tile(i), :]], axis=1)
        turned = product(x, rot[0])
        yy[0, tile(i), :] = turned[:, :128]
        yy[1, tile(i), :] = turned[:, 128:]
        return square(turned)

    def turn_own(i, carry):
        return carry[0] + turn_first(i), carry[1] + turn_second(i)

    square_c = turn_second(raw)
    forward(2 * raw).start()
    square_ab, square_c = lax.fori_loop(0, raw, turn_own, (turn_first(raw), square_c))
    diag[0:1, :] = square_ab[:, :128]
    diag[1:2, :] = square_ab[:, 128:]
    diag[2:3, :] = square_c
    keep = pltpu.make_async_copy(yy, y_ref, out_sem.at[0])

    def role_of(slot):
        return jnp.where(slot == a, 0, jnp.where(slot == b, 1, 2))

    a2, b2, c2 = (role_of(slot) for slot in roles(pairing_ref[1, yc]))
    gram_p = gram(lambda i: yy[a2, tile(i), :], lambda i: yy[b2, tile(i), :])
    lows = [diag[pl.ds(k, 1), :] for k in (a2, b2, c2)]

    for k in range(2 * raw):
        forward(k).wait_recv()

    def meet(i, block, carry):
        total, norms = carry
        return (
            total + product_of_rows(yy[c2, tile(i), :], block),
            norms + square(block),
        )

    def turn_and_meet(i, carry):
        x = jnp.concatenate([zc[tile(i), :], z3[tile(i), :]], axis=1)
        block = product(x, rot[2, :, 128:])
        z[tile(i), :] = block
        return meet(i, block, carry)

    met = lax.fori_loop(
        0, raw, turn_and_meet, (jnp.zeros((128, 128), F32), jnp.zeros((1, 128), F32))
    )
    forward(2 * raw).wait_recv()
    gram_q, last = meet(raw, z[tile(raw), :], met)
    keep_z = pltpu.make_async_copy(z, z_ref, out_sem.at[1])
    for k in range(raw):
        forward(k).wait_send()

    def backward(k):
        part = (upper, lower)[k]
        return pltpu.make_async_remote_copy(
            src_ref=q.at[part], dst_ref=qn_ref.at[part], send_sem=q_send.at[k], recv_sem=q_recv.at[k],
            device_id=(yr, before), device_id_type=MESH,
        )

    def early_second():
        q[upper, :] = yy[c2, upper, :]
        backward(0).start()
        q[lower, :] = yy[c2, lower, :]
        keep.start()
        keep_z.start()

    first, second, third = summed(
        1, gram_p, gram_q, (*lows, last), early_second, lambda: backward(1).start()
    )
    turns = rotations((first, second, third), state, weight)
    turn_ref[:128, 0:128] = turns[0][0]
    turn_ref[:128, 128:256] = turns[0][1]
    turn_ref[128:, 0:128] = turns[0][2]
    turn_ref[128:, 128:256] = turns[0][3]
    turn_ref[:128, 256:384] = turns[1][0]
    turn_ref[128:, 256:384] = turns[1][2]
    turn_ref[:128, 384:512] = turns[2][1]
    turn_ref[128:, 384:512] = turns[2][3]

    keep.wait()
    keep_z.wait()
    for k in range(raw, 2 * raw + 1):
        forward(k).wait_send()
    for k in range(2):
        backward(k).wait()
    for s in range(4):
        whole = recv.at[s, pl.ds(0, ALL - 1)]
        pltpu.make_async_copy(whole, whole, a2a_send).wait()
    for t in range(2):
        whole = arrived.at[t, pl.ds(0, ROWS - 1)]
        pltpu.make_async_copy(whole, whole, rs_send.at[t]).wait()
        whole = coup.at[t, pl.ds(0, ROWS - 1)]
        pltpu.make_async_copy(whole, whole, ag_send.at[t]).wait()

    @pl.when(yr >= 16)
    def _():
        for t in range(2):
            whole = coup.at[t]
            pltpu.make_async_copy(whole, whole, lend_send.at[t]).wait()


def two_steps(v, order, pairing):
    dma = pltpu.SemaphoreType.DMA
    return pl.pallas_call(
        steps_kernel,
        out_shape=(
            jax.ShapeDtypeStruct((4, PIX, 128), F32),
            jax.ShapeDtypeStruct((PIX, 128), F32),
            jax.ShapeDtypeStruct((PIX, 128), F32),
            jax.ShapeDtypeStruct((256, 512), F32),
        ),
        in_specs=[ANY, SMEM, SMEM],
        out_specs=(ANY, ANY, ANY, pl.BlockSpec(memory_space=pltpu.VMEM)),
        scratch_shapes=[
            pltpu.VMEM((8192, 128), F32),
            pltpu.VMEM((8, 2, ROWS, 16, 128), F32),
            pltpu.VMEM((4, ALL, 16, 128), F32),
            pltpu.VMEM((4, PIX, 128), F32),
            pltpu.VMEM((4, PIX, 128), F32),
            pltpu.VMEM((4, PIX, 128), F32),
            pltpu.VMEM((PIX, 128), F32),
            pltpu.VMEM((PIX, 128), F32),
            pltpu.VMEM((PIX, 128), F32),
            pltpu.VMEM((PIX, 128), F32),
            pltpu.VMEM((4, 128), F32),
            pltpu.VMEM((2, ROWS, 10, 128), F32),
            pltpu.VMEM((2, ROWS, 10, 128), F32),
            pltpu.VMEM((2, 8, 128), F32),
            pltpu.VMEM((2, ROWS, 8, 128), F32),
            pltpu.VMEM((2, 16, 8, 128), F32),
            pltpu.VMEM((3, 256, 256), F32),
            pltpu.VMEM((6, 256, 128), F32),
            pltpu.VMEM((6, 128, 128), F32),
            dma((8,)), dma((2,)), dma, dma((4,)), dma((2,)), dma((2,)), dma((2,)), dma((2,)), dma((2,)), dma((2,)),
            dma((2 * TILES - 1,)), dma((2 * TILES - 1,)), dma((2,)), dma((2,)),
        ],
        compiler_params=pltpu.CompilerParams(
            collective_id=0, has_side_effects=True, vmem_limit_bytes=VMEM
        ),
    )(v, order, pairing)


def finish_kernel(y_ref, z_ref, qn_ref, turn_ref, pairing_ref, out_ref):
    yc = lax.axis_index("cols")
    a, b, c = roles(pairing_ref[0, yc])
    slots = roles(pairing_ref[1, yc])
    a2, b2, c2 = (jnp.where(slot == a, 0, jnp.where(slot == b, 1, 2)) for slot in slots)
    at = [pl.ds(pl.multiple_of(slot * 128, 128), 128) for slot in slots]
    here = tile(pl.program_id(0))

    def turned(first, second, columns):
        return product(jnp.concatenate([first[here, :], second[here, :]], axis=1), turn_ref[:, columns])

    pair = turned(y_ref.at[a2], y_ref.at[b2], pl.ds(0, 256))
    out_ref[:, at[0]] = pair[:, :128]
    out_ref[:, at[1]] = pair[:, 128:]
    out_ref[:, at[2]] = turned(y_ref.at[c2], z_ref, pl.ds(256, 128))
    out_ref[:, 384:512] = turned(qn_ref, y_ref.at[3], pl.ds(384, 128))


def finish(y, z, qn, turn, pairing):
    rows = TILE
    return pl.pallas_call(
        finish_kernel,
        grid=(PIX // rows,),
        out_shape=jax.ShapeDtypeStruct((PIX, 512), F32),
        in_specs=[INNER, INNER, INNER, INNER, SMEM],
        out_specs=pl.BlockSpec((rows, 512), lambda i: (i, 0)),
        compiler_params=pltpu.CompilerParams(vmem_limit_bytes=24 * 2**20),
    )(y, z, qn, turn, pairing)


def body(tracks, pixel_order, pairing):
    v = tracks.reshape(8, 2, 512, 128).transpose(0, 2, 1, 3).reshape(8192, 128)
    return finish(*two_steps(v, pixel_order, pairing), pairing)


def solution(mesh):
    placed = (P(("rows", "cols"), None, None), P("rows"), P())
    return jax.shard_map(
        body, mesh=mesh, in_specs=placed, out_specs=P("rows", "cols"), check_vma=False
    )
```

```python
import jax
import jax.numpy as jnp
from jax import lax
from jax.experimental import pallas as pl
from jax.experimental.pallas import tpu as pltpu
from jax.sharding import PartitionSpec as P

F32 = jnp.float32
MESH = pl.DeviceIdType.MESH
ANY = pl.BlockSpec(memory_space=pl.ANY)
SMEM = pl.BlockSpec(memory_space=pltpu.SMEM)
INNER = pl.BlockSpec(memory_space=pltpu.VMEM)
HIGH = lax.Precision.HIGH
NS_STEPS = 6
ROWS = 32
COLS = 4
ALL = ROWS * COLS
PIX = 2048
TILE = 512
TILES = PIX // TILE
VMEM = 46 * 2**20


def product(a, b):
    return jnp.dot(a, b, precision=HIGH, preferred_element_type=F32)


def product_of_rows(a, b):
    return lax.dot_general(a, b, (((0,), (0,)), ((), ())), precision=HIGH, preferred_element_type=F32)


def any_peer(i, yr, yc):
    first, second, third = (i >> 1) & 3, (i >> 3) & 3, i >> 5
    y = ((yr >> 3) + first + second) & 3
    x = (((yr >> 1) & 2) + (yc >> 1) + first) & 3
    z = (yr + first + third + 2 * second) & 3
    return (y << 3) + ((x >> 1) << 2) + z, ((x & 1) << 1) + ((yc + i) & 1)


def row_peer(i, yr):
    y = ((yr >> 3) + (i >> 2)) & 3
    x = ((yr >> 2) + (i >> 4)) & 1
    z = (yr + i) & 3
    return (y << 3) + (x << 2) + z


def hops(i):
    ring = (0, 1, 2, 1)
    return ring[i & 3] + ring[i >> 2 & 3] + 2 * (i >> 4)


FAR_FIRST = sorted(range(ROWS), key=hops, reverse=True)


def roles(choice):
    low = jnp.where(choice == 2, 1, 0)
    high = jnp.where(choice == 0, 1, 2)
    return low, high, 2 - choice


def tile(i):
    if isinstance(i, int):
        return pl.ds(i * TILE, TILE)
    return pl.ds(pl.multiple_of(i * TILE, TILE), TILE)


def exact(a, b):
    return jnp.dot(a, b, precision=lax.Precision.HIGHEST, preferred_element_type=F32)


def rotations(couplings, state, weight):
    size = 128
    row = lax.broadcasted_iota(jnp.int32, (size, size), 0)
    col = lax.broadcasted_iota(jnp.int32, (size, size), 1)
    eye = jnp.where(row == col, 1.0, 0.0).astype(F32)
    count = 2 * len(couplings)
    flipped = [c.T for c in couplings]
    for k, c in enumerate(couplings):
        total = 1.0 + jnp.sum(jnp.sum(c * c, axis=1, keepdims=True), axis=0, keepdims=True)
        start = eye * (1.0 / jnp.sqrt(total))
        for m, square in ((2 * k, exact(c, flipped[k])), (2 * k + 1, exact(flipped[k], c))):
            weight[m] = eye + square
            state[m, :size, :] = (eye + square) / total
            state[m, size:, :] = start

    def step(_, carry):
        held = [state[m] for m in range(count)]
        factors = [1.5 * eye - 0.5 * h[:size] for h in held]
        once = [product(h, f) for h, f in zip(held, factors)]
        twice = [product(o[:size], f) for o, f in zip(once, factors)]
        for m in range(count):
            state[m, :size, :] = twice[m]
            state[m, size:, :] = once[m][size:]
        return carry

    lax.fori_loop(0, NS_STEPS - 1, step, 0, unroll=True)
    half = [state[m, size:, :] for m in range(count)]
    met = [exact(weight[m], half[m]) for m in range(count)]
    inner = [exact(half[m], met[m]) for m in range(count)]
    crossed = [exact(half[2 * k], c) for k, c in enumerate(couplings)]
    factors = [1.5 * eye - 0.5 * n for n in inner]
    last = [exact(h, f) for h, f in zip(half, factors)]
    out = []
    for k in range(len(couplings)):
        cross = exact(factors[2 * k], crossed[k])
        out.append((last[2 * k], cross, -cross.T, last[2 * k + 1]))
    return out


def steps_kernel(
    v_ref, order_ref, pairing_ref, y_ref, z_ref, qn_ref, turn_ref,
    vv, send, recv, flat, xt, yy, zc, z3, z, q, diag, parts, arrived, own, coup, coupn, rot, state, weight,
    load_sem, out_sem, a2a_send, a2a_recv, rs_send, rs_recv, ag_send, ag_recv, lend_send, lend_recv,
    z_send, z_recv, q_send, q_recv,
):
    yr, yc = lax.axis_index("rows"), lax.axis_index("cols")
    me = yr * COLS + yc
    after, before = (yc + 1) & 3, (yc + 3) & 3
    barrier = pltpu.get_barrier_semaphore()

    def load(frame):
        lines = pl.ds(frame * 1024, 1024)
        return pltpu.make_async_copy(v_ref.at[lines], vv.at[lines], load_sem.at[frame])

    for s in range(4):
        load(s).start()
        load(4 + s).start()

    def greet(i, carry):
        pl.semaphore_signal(barrier, inc=1, device_id=any_peer(i, yr, yc), device_id_type=MESH)
        return carry

    lax.fori_loop(1, ALL, greet, 0, unroll=9)
    for s in range(4):
        load(s).wait()
        load(4 + s).wait()

        def split(block, carry, s=s):
            for frame in (s, 4 + s):
                for part in range(2):
                    send[frame, part, block] = vv[pl.ds(frame * 1024 + block * 32 + part, 16, stride=2), :]
            return carry

        lax.fori_loop(0, ROWS, split, 0, unroll=2)
        if s == 0:
            pl.semaphore_wait(barrier, ALL - 1)

        def scatter(i, carry, s=s):
            r, c = any_peer(i, yr, yc)
            pltpu.make_async_remote_copy(
                src_ref=send.at[((c & 1) << 2) + s, c >> 1, r], dst_ref=recv.at[s, me],
                send_sem=a2a_send, recv_sem=a2a_recv.at[s],
                device_id=(r, c), device_id_type=MESH,
            ).start()
            return carry

        lax.fori_loop(1, ALL, scatter, 0)
        recv[s, me] = send[((yc & 1) << 2) + s, yc >> 1, yr]

    def gram(left, right):
        def add(i, carry):
            return carry + product_of_rows(left(i), right(i))

        return lax.fori_loop(0, TILES, add, jnp.zeros((128, 128), F32))

    def squares(block):
        def add(i, carry):
            x = block(i)
            return carry + jnp.sum(x * x, axis=0, keepdims=True)

        return lax.fori_loop(0, TILES, add, jnp.zeros((1, 128), F32))

    def place(s):
        def move(i, carry):
            for u in range(16):
                k = i * 16 + u
                xt[s, pl.ds(k, 1), :] = flat[s, pl.ds(order_ref[k] & (PIX - 1), 1), :]
            return carry

        lax.fori_loop(0, PIX // 16, move, 0)

    owns_first = (yr & 1) == 0

    def deal(t, p, cross, diagonals):
        low = jnp.concatenate(diagonals, axis=0)
        for k in range(16):
            parts[t, 2 * k + p, 0:8, :] = cross[8 * k : 8 * k + 8]
            parts[t, 2 * k + p, 8:10, :] = low
        odd = (yr + p) & 1

        def give(m):
            r = row_peer(2 * m + odd, yr)
            pltpu.make_async_remote_copy(
                src_ref=parts.at[t, r], dst_ref=arrived.at[t, yr],
                send_sem=rs_send.at[t], recv_sem=rs_recv.at[t],
                device_id=(r, yc), device_id_type=MESH,
            ).start()

        for m in sorted(range(1, 16), key=lambda m: hops(2 * m + 1), reverse=True):
            give(m)

        @pl.when(odd == 1)
        def _():
            give(0)

        @pl.when(odd == 0)
        def _():
            arrived[t, yr] = parts[t, yr]

    def own_part(t, p):
        whole = arrived.at[t, pl.ds(0, ROWS - 1)]
        pltpu.make_async_copy(whole, whole, rs_recv.at[t]).wait()
        total = arrived[t, 0]
        for r in range(1, ROWS):
            total = total + arrived[t, r]
        left, right = total[8:9], total[9:10]
        spot = lax.broadcasted_iota(jnp.int32, (8, 128), 0) + 8 * (yr >> 1)
        lane = lax.broadcasted_iota(jnp.int32, (8, 128), 1)
        left = jnp.sum(jnp.where(spot == lane, jnp.broadcast_to(left, (8, 128)), 0.0), axis=1, keepdims=True)
        mine = total[0:8] / (left + right)
        own[t] = mine
        coup[t, p, yr >> 1] = mine
        for i in FAR_FIRST[:-1]:
            pltpu.make_async_remote_copy(
                src_ref=own.at[t], dst_ref=coup.at[t, p, yr >> 1],
                send_sem=ag_send.at[t], recv_sem=ag_recv.at[2 * t + p],
                device_id=(row_peer(i, yr), yc), device_id_type=MESH,
            ).start()
        if p == 1:
            for i in FAR_FIRST:
                pltpu.make_async_remote_copy(
                    src_ref=own.at[t], dst_ref=coupn.at[t, yr >> 1],
                    send_sem=lend_send.at[t], recv_sem=lend_recv.at[t],
                    device_id=(row_peer(i, yr), before if t else after), device_id_type=MESH,
                ).start()

    def shared(t, p):
        mine = (yr & 1) == p
        for count, chosen in ((15, mine), (16, jnp.logical_not(mine))):
            @pl.when(chosen)
            def _(count=count):
                whole = coup.at[t, p, pl.ds(0, count)]
                pltpu.make_async_copy(whole, whole, ag_recv.at[2 * t + p]).wait()

        return coup[t, p].reshape(128, 128)

    def lent(t):
        whole = coupn.at[t]
        pltpu.make_async_copy(whole, whole, lend_recv.at[t]).wait()
        return coupn[t].reshape(128, 128)

    a, b, c = roles(pairing_ref[0, yc])
    for s in range(4):
        if s == 3:
            gram_p = gram(lambda i: flat[a, tile(i), :], lambda i: flat[b, tile(i), :])
            deal(0, 0, gram_p, (diag[pl.ds(a, 1), :], diag[pl.ds(b, 1), :]))
        whole = recv.at[s, pl.ds(0, ALL - 1)]
        pltpu.make_async_copy(whole, whole, a2a_recv.at[s]).wait()
        for g in range(16):
            flat[s, pl.ds(g * 128, 128), :] = recv[s, :, g, :].T
        diag[pl.ds(s, 1), :] = squares(lambda i, s=s: flat[s, tile(i), :])
        if s < 3:
            place(s)

    raw = TILES - 1

    def forward(k):
        at = pl.ds(k % raw * TILE, TILE)
        pairs = ((q.at[at], zc.at[at]), (xt.at[3, at], z3.at[at]))
        src, dst = pairs[k // raw] if k < 2 * raw else (yy.at[3, pl.ds(raw * TILE, TILE)], z.at[pl.ds(raw * TILE, TILE)])
        return pltpu.make_async_remote_copy(
            src_ref=src, dst_ref=dst, send_sem=z_send.at[k], recv_sem=z_recv.at[k],
            device_id=(yr, after), device_id_type=MESH,
        )

    q[pl.ds(0, TILE), :] = xt[c, pl.ds(0, TILE), :]
    forward(0).start()
    gram_q = gram(lambda i: flat[c, tile(i), :], lambda i: flat[3, tile(i), :])

    deal(0, 1, gram_q, (diag[pl.ds(c, 1), :], diag[3:4, :]))

    @pl.when(owns_first)
    def _():
        own_part(0, 0)

    for k in range(1, raw):
        q[pl.ds(k * TILE, TILE), :] = xt[c, pl.ds(k * TILE, TILE), :]
        forward(k).start()
    place(3)

    @pl.when(jnp.logical_not(owns_first))
    def _():
        own_part(0, 1)

    for k in range(raw, 2 * raw):
        forward(k).start()

    def keep_rotation(k, parts_of):
        top, cross, down, low = parts_of
        rot[k, :128, :128] = top
        rot[k, :128, 128:] = cross
        rot[k, 128:, :128] = down
        rot[k, 128:, 128:] = low

    def square(x):
        return jnp.sum(x * x, axis=0, keepdims=True)

    def turn_second(i):
        x = jnp.concatenate([xt[c, tile(i), :], xt[3, tile(i), :]], axis=1)
        turned = product(x, rot[1])
        yy[3, tile(i), :] = turned[:, 128:]
        yy[2, tile(i), :] = turned[:, :128]
        return square(turned[:, :128])

    def turn_first(i):
        x = jnp.concatenate([xt[a, tile(i), :], xt[b, tile(i), :]], axis=1)
        turned = product(x, rot[0])
        yy[0, tile(i), :] = turned[:, :128]
        yy[1, tile(i), :] = turned[:, 128:]
        return square(turned)

    keep_rotation(0, rotations((shared(0, 0),), state, weight)[0])
    square_ab = lax.fori_loop(
        0, TILES, lambda i, carry: carry + turn_first(i), jnp.zeros((1, 256), F32)
    )
    for k, turn in enumerate(rotations((shared(0, 1), lent(0)), state, weight)):
        keep_rotation(1 + k, turn)
    square_c = turn_second(raw)
    forward(2 * raw).start()
    square_c = lax.fori_loop(0, raw, lambda i, carry: carry + turn_second(i), square_c)
    diag[0:1, :] = square_ab[:, :128]
    diag[1:2, :] = square_ab[:, 128:]
    diag[2:3, :] = square_c
    keep = pltpu.make_async_copy(yy, y_ref, out_sem.at[0])

    def role_of(slot):
        return jnp.where(slot == a, 0, jnp.where(slot == b, 1, 2))

    a2, b2, c2 = (role_of(slot) for slot in roles(pairing_ref[1, yc]))
    gram_p = gram(lambda i: yy[a2, tile(i), :], lambda i: yy[b2, tile(i), :])
    deal(1, 0, gram_p, (diag[pl.ds(a2, 1), :], diag[pl.ds(b2, 1), :]))

    for k in range(2 * raw):
        forward(k).wait_recv()

    def meet(i, block, carry):
        total, norms = carry
        return (
            total + product_of_rows(yy[c2, tile(i), :], block),
            norms + square(block),
        )

    def turn_and_meet(i, carry):
        x = jnp.concatenate([zc[tile(i), :], z3[tile(i), :]], axis=1)
        block = product(x, rot[2, :, 128:])
        z[tile(i), :] = block
        return meet(i, block, carry)

    met = lax.fori_loop(
        0, raw, turn_and_meet, (jnp.zeros((128, 128), F32), jnp.zeros((1, 128), F32))
    )
    forward(2 * raw).wait_recv()
    gram_q, last = meet(raw, z[tile(raw), :], met)
    keep_z = pltpu.make_async_copy(z, z_ref, out_sem.at[1])
    for k in range(raw):
        forward(k).wait_send()

    def backward(k):
        part = tile(k)
        return pltpu.make_async_remote_copy(
            src_ref=q.at[part], dst_ref=qn_ref.at[part], send_sem=q_send.at[k], recv_sem=q_recv.at[k],
            device_id=(yr, before), device_id_type=MESH,
        )

    deal(1, 1, gram_q, (diag[pl.ds(c2, 1), :], last))
    for k in range(TILES):
        q[tile(k), :] = yy[c2, tile(k), :]
    backward(0).start()

    @pl.when(owns_first)
    def _():
        own_part(1, 0)
        backward(1).start()

    @pl.when(jnp.logical_not(owns_first))
    def _():
        backward(1).start()
        own_part(1, 1)

    for k in range(2, TILES):
        backward(k).start()
    keep.start()
    keep_z.start()
    turns = rotations((shared(1, 0),), state, weight)
    turns += rotations((shared(1, 1), lent(1)), state, weight)
    turn_ref[:128, 0:128] = turns[0][0]
    turn_ref[:128, 128:256] = turns[0][1]
    turn_ref[128:, 0:128] = turns[0][2]
    turn_ref[128:, 128:256] = turns[0][3]
    turn_ref[:128, 256:384] = turns[1][0]
    turn_ref[128:, 256:384] = turns[1][2]
    turn_ref[:128, 384:512] = turns[2][1]
    turn_ref[128:, 384:512] = turns[2][3]

    keep.wait()
    keep_z.wait()
    for k in range(raw, 2 * raw + 1):
        forward(k).wait_send()
    for k in range(TILES):
        backward(k).wait()
    for s in range(4):
        whole = recv.at[s, pl.ds(0, ALL - 1)]
        pltpu.make_async_copy(whole, whole, a2a_send).wait()
    for t in range(2):
        whole = arrived.at[t, pl.ds(0, ROWS - 1)]
        pltpu.make_async_copy(whole, whole, rs_send.at[t]).wait()
        whole = flat.at[0, pl.ds(0, 8 * (ROWS - 1))]
        pltpu.make_async_copy(whole, whole, ag_send.at[t]).wait()

    @pl.when(jnp.logical_not(owns_first))
    def _():
        for t in range(2):
            whole = flat.at[0, pl.ds(0, 8 * ROWS)]
            pltpu.make_async_copy(whole, whole, lend_send.at[t]).wait()


def two_steps(v, order, pairing):
    dma = pltpu.SemaphoreType.DMA
    return pl.pallas_call(
        steps_kernel,
        out_shape=(
            jax.ShapeDtypeStruct((4, PIX, 128), F32),
            jax.ShapeDtypeStruct((PIX, 128), F32),
            jax.ShapeDtypeStruct((PIX, 128), F32),
            jax.ShapeDtypeStruct((256, 512), F32),
        ),
        in_specs=[ANY, SMEM, SMEM],
        out_specs=(ANY, ANY, ANY, pl.BlockSpec(memory_space=pltpu.VMEM)),
        scratch_shapes=[
            pltpu.VMEM((8192, 128), F32),
            pltpu.VMEM((8, 2, ROWS, 16, 128), F32),
            pltpu.VMEM((4, ALL, 16, 128), F32),
            pltpu.VMEM((4, PIX, 128), F32),
            pltpu.VMEM((4, PIX, 128), F32),
            pltpu.VMEM((4, PIX, 128), F32),
            pltpu.VMEM((PIX, 128), F32),
            pltpu.VMEM((PIX, 128), F32),
            pltpu.VMEM((PIX, 128), F32),
            pltpu.VMEM((PIX, 128), F32),
            pltpu.VMEM((4, 128), F32),
            pltpu.VMEM((2, ROWS, 10, 128), F32),
            pltpu.VMEM((2, ROWS, 10, 128), F32),
            pltpu.VMEM((2, 8, 128), F32),
            pltpu.VMEM((2, 2, 16, 8, 128), F32),
            pltpu.VMEM((2, 16, 8, 128), F32),
            pltpu.VMEM((3, 256, 256), F32),
            pltpu.VMEM((6, 256, 128), F32),
            pltpu.VMEM((6, 128, 128), F32),
            dma((8,)), dma((2,)), dma, dma((4,)), dma((2,)), dma((2,)), dma((2,)), dma((4,)), dma((2,)), dma((2,)),
            dma((2 * TILES - 1,)), dma((2 * TILES - 1,)), dma((TILES,)), dma((TILES,)),
        ],
        compiler_params=pltpu.CompilerParams(
            collective_id=0, has_side_effects=True, vmem_limit_bytes=VMEM
        ),
    )(v, order, pairing)


def finish_kernel(y_ref, z_ref, qn_ref, turn_ref, pairing_ref, out_ref):
    yc = lax.axis_index("cols")
    a, b, c = roles(pairing_ref[0, yc])
    slots = roles(pairing_ref[1, yc])
    a2, b2, c2 = (jnp.where(slot == a, 0, jnp.where(slot == b, 1, 2)) for slot in slots)
    at = [pl.ds(pl.multiple_of(slot * 128, 128), 128) for slot in slots]
    here = tile(pl.program_id(0))

    def turned(first, second, columns):
        return product(jnp.concatenate([first[here, :], second[here, :]], axis=1), turn_ref[:, columns])

    pair = turned(y_ref.at[a2], y_ref.at[b2], pl.ds(0, 256))
    out_ref[:, at[0]] = pair[:, :128]
    out_ref[:, at[1]] = pair[:, 128:]
    out_ref[:, at[2]] = turned(y_ref.at[c2], z_ref, pl.ds(256, 128))
    out_ref[:, 384:512] = turned(qn_ref, y_ref.at[3], pl.ds(384, 128))


def finish(y, z, qn, turn, pairing):
    rows = TILE
    return pl.pallas_call(
        finish_kernel,
        grid=(PIX // rows,),
        out_shape=jax.ShapeDtypeStruct((PIX, 512), F32),
        in_specs=[INNER, INNER, INNER, INNER, SMEM],
        out_specs=pl.BlockSpec((rows, 512), lambda i: (i, 0)),
        compiler_params=pltpu.CompilerParams(vmem_limit_bytes=24 * 2**20),
    )(y, z, qn, turn, pairing)


def body(tracks, pixel_order, pairing):
    v = tracks.reshape(8, 2, 512, 128).transpose(0, 2, 1, 3).reshape(8192, 128)
    return finish(*two_steps(v, pixel_order, pairing), pairing)


def solution(mesh):
    placed = (P(("rows", "cols"), None, None), P("rows"), P())
    return jax.shard_map(
        body, mesh=mesh, in_specs=placed, out_specs=P("rows", "cols"), check_vma=False
    )
```

```python
import jax
import jax.numpy as jnp
from jax import lax
from jax.experimental import pallas as pl
from jax.experimental.pallas import tpu as pltpu
from jax.sharding import PartitionSpec as P

F32 = jnp.float32
MESH = pl.DeviceIdType.MESH
ANY = pl.BlockSpec(memory_space=pl.ANY)
SMEM = pl.BlockSpec(memory_space=pltpu.SMEM)
INNER = pl.BlockSpec(memory_space=pltpu.VMEM)
HIGH = lax.Precision.HIGH
NS_STEPS = 6
ROWS = 32
COLS = 4
ALL = ROWS * COLS
PIX = 2048
TILE = 512
TILES = PIX // TILE
VMEM = 46 * 2**20


def product(a, b):
    return jnp.dot(a, b, precision=HIGH, preferred_element_type=F32)


def product_of_rows(a, b):
    return lax.dot_general(a, b, (((0,), (0,)), ((), ())), precision=HIGH, preferred_element_type=F32)


def any_peer(i, yr, yc):
    first, second, third = (i >> 1) & 3, (i >> 3) & 3, i >> 5
    y = ((yr >> 3) + first + second) & 3
    x = (((yr >> 1) & 2) + (yc >> 1) + first) & 3
    z = (yr + first + third + 2 * second) & 3
    return (y << 3) + ((x >> 1) << 2) + z, ((x & 1) << 1) + ((yc + i) & 1)


def row_peer(i, yr):
    y = ((yr >> 3) + (i >> 2)) & 3
    x = ((yr >> 2) + (i >> 4)) & 1
    z = (yr + i) & 3
    return (y << 3) + (x << 2) + z


def hops(i):
    ring = (0, 1, 2, 1)
    return ring[i & 3] + ring[i >> 2 & 3] + 2 * (i >> 4)


FAR_FIRST = sorted(range(ROWS), key=hops, reverse=True)


def roles(choice):
    low = jnp.where(choice == 2, 1, 0)
    high = jnp.where(choice == 0, 1, 2)
    return low, high, 2 - choice


def tile(i):
    if isinstance(i, int):
        return pl.ds(i * TILE, TILE)
    return pl.ds(pl.multiple_of(i * TILE, TILE), TILE)


def exact(a, b):
    return jnp.dot(a, b, precision=lax.Precision.HIGHEST, preferred_element_type=F32)


def rotations(couplings, state, weight):
    size = 128
    row = lax.broadcasted_iota(jnp.int32, (size, size), 0)
    col = lax.broadcasted_iota(jnp.int32, (size, size), 1)
    eye = jnp.where(row == col, 1.0, 0.0).astype(F32)
    count = 2 * len(couplings)
    flipped = [c.T for c in couplings]
    for k, c in enumerate(couplings):
        total = 1.0 + jnp.sum(jnp.sum(c * c, axis=1, keepdims=True), axis=0, keepdims=True)
        start = eye * (1.0 / jnp.sqrt(total))
        for m, square in ((2 * k, exact(c, flipped[k])), (2 * k + 1, exact(flipped[k], c))):
            weight[m] = eye + square
            state[m, :size, :] = (eye + square) / total
            state[m, size:, :] = start

    def step(_, carry):
        held = [state[m] for m in range(count)]
        factors = [1.5 * eye - 0.5 * h[:size] for h in held]
        once = [product(h, f) for h, f in zip(held, factors)]
        twice = [product(o[:size], f) for o, f in zip(once, factors)]
        for m in range(count):
            state[m, :size, :] = twice[m]
            state[m, size:, :] = once[m][size:]
        return carry

    lax.fori_loop(0, NS_STEPS - 1, step, 0, unroll=True)
    half = [state[m, size:, :] for m in range(count)]
    met = [exact(weight[m], half[m]) for m in range(count)]
    inner = [exact(half[m], met[m]) for m in range(count)]
    crossed = [exact(half[2 * k], c) for k, c in enumerate(couplings)]
    factors = [1.5 * eye - 0.5 * n for n in inner]
    last = [exact(h, f) for h, f in zip(half, factors)]
    out = []
    for k in range(len(couplings)):
        cross = exact(factors[2 * k], crossed[k])
        out.append((last[2 * k], cross, -cross.T, last[2 * k + 1]))
    return out


def steps_kernel(
    v_ref, order_ref, pairing_ref, y_ref, z_ref, qn_ref, turn_ref,
    vv, send, recv, flat, xt, yy, zc, z3, z, q, diag, parts, arrived, own, coup, coupn, rot, state, weight,
    load_sem, out_sem, a2a_send, a2a_recv, rs_send, rs_recv, ag_send, ag_recv, lend_send, lend_recv,
    z_send, z_recv, q_send, q_recv,
):
    yr, yc = lax.axis_index("rows"), lax.axis_index("cols")
    me = yr * COLS + yc
    after, before = (yc + 1) & 3, (yc + 3) & 3
    barrier = pltpu.get_barrier_semaphore()

    def load(frame):
        lines = pl.ds(frame * 1024, 1024)
        return pltpu.make_async_copy(v_ref.at[lines], vv.at[lines], load_sem.at[frame])

    for s in range(4):
        load(s).start()
        load(4 + s).start()

    def greet(i, carry):
        pl.semaphore_signal(barrier, inc=1, device_id=any_peer(i, yr, yc), device_id_type=MESH)
        return carry

    lax.fori_loop(1, ALL, greet, 0, unroll=9)
    for s in range(4):
        load(s).wait()
        load(4 + s).wait()

        def split(block, carry, s=s):
            for frame in (s, 4 + s):
                for part in range(2):
                    send[frame, part, block] = vv[pl.ds(frame * 1024 + block * 32 + part, 16, stride=2), :]
            return carry

        lax.fori_loop(0, ROWS, split, 0, unroll=2)
        if s == 0:
            pl.semaphore_wait(barrier, ALL - 1)

        def scatter(i, carry, s=s):
            r, c = any_peer(i, yr, yc)
            pltpu.make_async_remote_copy(
                src_ref=send.at[((c & 1) << 2) + s, c >> 1, r], dst_ref=recv.at[s, me],
                send_sem=a2a_send, recv_sem=a2a_recv.at[s],
                device_id=(r, c), device_id_type=MESH,
            ).start()
            return carry

        lax.fori_loop(1, ALL, scatter, 0)
        recv[s, me] = send[((yc & 1) << 2) + s, yc >> 1, yr]

    def gram(left, right):
        def add(i, carry):
            return carry + product_of_rows(left(i), right(i))

        return lax.fori_loop(0, TILES, add, jnp.zeros((128, 128), F32), unroll=True)

    def squares(block):
        def add(i, carry):
            x = block(i)
            return carry + jnp.sum(x * x, axis=0, keepdims=True)

        return lax.fori_loop(0, TILES, add, jnp.zeros((1, 128), F32))

    def place(s):
        def move(i, carry):
            for u in range(16):
                k = i * 16 + u
                xt[s, pl.ds(k, 1), :] = flat[s, pl.ds(order_ref[k] & (PIX - 1), 1), :]
            return carry

        lax.fori_loop(0, PIX // 16, move, 0)

    owns_first = (yr & 1) == 0

    def deal(t, p, cross, diagonals):
        low = jnp.concatenate(diagonals, axis=0)
        for k in range(16):
            parts[t, 2 * k + p, 0:8, :] = cross[8 * k : 8 * k + 8]
            parts[t, 2 * k + p, 8:10, :] = low
        odd = (yr + p) & 1

        def give(m):
            r = row_peer(2 * m + odd, yr)
            pltpu.make_async_remote_copy(
                src_ref=parts.at[t, r], dst_ref=arrived.at[t, yr],
                send_sem=rs_send.at[t], recv_sem=rs_recv.at[t],
                device_id=(r, yc), device_id_type=MESH,
            ).start()

        for m in sorted(range(1, 16), key=lambda m: hops(2 * m + 1), reverse=True):
            give(m)

        @pl.when(odd == 1)
        def _():
            give(0)

        @pl.when(odd == 0)
        def _():
            arrived[t, yr] = parts[t, yr]

    def own_part(t, p):
        whole = arrived.at[t, pl.ds(0, ROWS - 1)]
        pltpu.make_async_copy(whole, whole, rs_recv.at[t]).wait()
        total = arrived[t, 0]
        for r in range(1, ROWS):
            total = total + arrived[t, r]
        left, right = total[8:9], total[9:10]
        spot = lax.broadcasted_iota(jnp.int32, (8, 128), 0) + 8 * (yr >> 1)
        lane = lax.broadcasted_iota(jnp.int32, (8, 128), 1)
        left = jnp.sum(jnp.where(spot == lane, jnp.broadcast_to(left, (8, 128)), 0.0), axis=1, keepdims=True)
        mine = total[0:8] / (left + right)
        own[t] = mine
        coup[t, p, yr >> 1] = mine
        for i in FAR_FIRST[:-1]:
            pltpu.make_async_remote_copy(
                src_ref=own.at[t], dst_ref=coup.at[t, p, yr >> 1],
                send_sem=ag_send.at[t], recv_sem=ag_recv.at[2 * t + p],
                device_id=(row_peer(i, yr), yc), device_id_type=MESH,
            ).start()
        if p == 1:
            for i in FAR_FIRST:
                pltpu.make_async_remote_copy(
                    src_ref=own.at[t], dst_ref=coupn.at[t, yr >> 1],
                    send_sem=lend_send.at[t], recv_sem=lend_recv.at[t],
                    device_id=(row_peer(i, yr), before if t else after), device_id_type=MESH,
                ).start()

    def shared(t, p):
        mine = (yr & 1) == p
        for count, chosen in ((15, mine), (16, jnp.logical_not(mine))):
            @pl.when(chosen)
            def _(count=count):
                whole = coup.at[t, p, pl.ds(0, count)]
                pltpu.make_async_copy(whole, whole, ag_recv.at[2 * t + p]).wait()

        return coup[t, p].reshape(128, 128)

    def lent(t):
        whole = coupn.at[t]
        pltpu.make_async_copy(whole, whole, lend_recv.at[t]).wait()
        return coupn[t].reshape(128, 128)

    raw = TILES - 1

    def forward(k):
        at = pl.ds(k % raw * TILE, TILE)
        pairs = ((q.at[at], zc.at[at]), (xt.at[3, at], z3.at[at]))
        src, dst = pairs[k // raw] if k < 2 * raw else (yy.at[3, pl.ds(raw * TILE, TILE)], z.at[pl.ds(raw * TILE, TILE)])
        return pltpu.make_async_remote_copy(
            src_ref=src, dst_ref=dst, send_sem=z_send.at[k], recv_sem=z_recv.at[k],
            device_id=(yr, after), device_id_type=MESH,
        )

    def square(x):
        return jnp.sum(x * x, axis=0, keepdims=True)

    a, b, c = roles(pairing_ref[0, yc])
    for s in range(4):
        if s == 3:
            gram_p = gram(lambda i: flat[a, tile(i), :], lambda i: flat[b, tile(i), :])
            deal(0, 0, gram_p, (diag[pl.ds(a, 1), :], diag[pl.ds(b, 1), :]))
        whole = recv.at[s, pl.ds(0, ALL - 1)]
        pltpu.make_async_copy(whole, whole, a2a_recv.at[s]).wait()
        if s < 3:
            for g in range(16):
                flat[s, pl.ds(g * 128, 128), :] = recv[s, :, g, :].T
            diag[pl.ds(s, 1), :] = squares(lambda i, s=s: flat[s, tile(i), :])
            place(s)

    q[pl.ds(0, TILE), :] = xt[c, pl.ds(0, TILE), :]
    forward(0).start()
    gram_q = jnp.zeros((128, 128), F32)
    square_3 = jnp.zeros((1, 128), F32)
    span = TILE // 128
    for k in range(TILES):
        block = jnp.concatenate([recv[3, :, span * k + g, :].T for g in range(span)], axis=0)
        flat[3, tile(k), :] = block
        gram_q = gram_q + product_of_rows(flat[c, tile(k), :], block)
        square_3 = square_3 + square(block)

    deal(0, 1, gram_q, (diag[pl.ds(c, 1), :], square_3))

    @pl.when(owns_first)
    def _():
        own_part(0, 0)

    for k in range(1, raw):
        q[pl.ds(k * TILE, TILE), :] = xt[c, pl.ds(k * TILE, TILE), :]
        forward(k).start()
    place(3)

    @pl.when(jnp.logical_not(owns_first))
    def _():
        own_part(0, 1)

    for k in range(raw, 2 * raw):
        forward(k).start()

    def keep_rotation(k, parts_of):
        top, cross, down, low = parts_of
        rot[k, :128, :128] = top
        rot[k, :128, 128:] = cross
        rot[k, 128:, :128] = down
        rot[k, 128:, 128:] = low

    def turn_second(i):
        x = jnp.concatenate([xt[c, tile(i), :], xt[3, tile(i), :]], axis=1)
        turned = product(x, rot[1])
        yy[3, tile(i), :] = turned[:, 128:]
        yy[2, tile(i), :] = turned[:, :128]
        return square(turned[:, :128])

    def turn_first(i):
        x = jnp.concatenate([xt[a, tile(i), :], xt[b, tile(i), :]], axis=1)
        turned = product(x, rot[0])
        yy[0, tile(i), :] = turned[:, :128]
        yy[1, tile(i), :] = turned[:, 128:]
        return square(turned)

    keep_rotation(0, rotations((shared(0, 0),), state, weight)[0])
    square_ab = lax.fori_loop(
        0, TILES, lambda i, carry: carry + turn_first(i), jnp.zeros((1, 256), F32)
    )
    for k, turn in enumerate(rotations((shared(0, 1), lent(0)), state, weight)):
        keep_rotation(1 + k, turn)
    square_c = turn_second(raw)
    forward(2 * raw).start()
    square_c = lax.fori_loop(0, raw, lambda i, carry: carry + turn_second(i), square_c, unroll=True)
    diag[0:1, :] = square_ab[:, :128]
    diag[1:2, :] = square_ab[:, 128:]
    diag[2:3, :] = square_c
    keep = pltpu.make_async_copy(yy, y_ref, out_sem.at[0])

    def role_of(slot):
        return jnp.where(slot == a, 0, jnp.where(slot == b, 1, 2))

    a2, b2, c2 = (role_of(slot) for slot in roles(pairing_ref[1, yc]))
    gram_p = gram(lambda i: yy[a2, tile(i), :], lambda i: yy[b2, tile(i), :])
    deal(1, 0, gram_p, (diag[pl.ds(a2, 1), :], diag[pl.ds(b2, 1), :]))

    for k in range(2 * raw):
        forward(k).wait_recv()

    def meet(i, block, carry):
        total, norms = carry
        return (
            total + product_of_rows(yy[c2, tile(i), :], block),
            norms + square(block),
        )

    def turn_and_meet(i, carry):
        x = jnp.concatenate([zc[tile(i), :], z3[tile(i), :]], axis=1)
        block = product(x, rot[2, :, 128:])
        z[tile(i), :] = block
        return meet(i, block, carry)

    met = lax.fori_loop(
        0, raw, turn_and_meet, (jnp.zeros((128, 128), F32), jnp.zeros((1, 128), F32)), unroll=True
    )
    forward(2 * raw).wait_recv()
    gram_q, last = meet(raw, z[tile(raw), :], met)
    keep_z = pltpu.make_async_copy(z, z_ref, out_sem.at[1])
    for k in range(raw):
        forward(k).wait_send()

    def backward(k):
        part = tile(k)
        return pltpu.make_async_remote_copy(
            src_ref=q.at[part], dst_ref=qn_ref.at[part], send_sem=q_send.at[k], recv_sem=q_recv.at[k],
            device_id=(yr, before), device_id_type=MESH,
        )

    deal(1, 1, gram_q, (diag[pl.ds(c2, 1), :], last))
    for k in range(TILES):
        q[tile(k), :] = yy[c2, tile(k), :]
    backward(0).start()

    @pl.when(owns_first)
    def _():
        own_part(1, 0)
        backward(1).start()

    @pl.when(jnp.logical_not(owns_first))
    def _():
        backward(1).start()
        own_part(1, 1)

    for k in range(2, TILES):
        backward(k).start()
    keep.start()
    keep_z.start()
    turns = rotations((shared(1, 0),), state, weight)
    turns += rotations((shared(1, 1), lent(1)), state, weight)
    turn_ref[:128, 0:128] = turns[0][0]
    turn_ref[:128, 128:256] = turns[0][1]
    turn_ref[128:, 0:128] = turns[0][2]
    turn_ref[128:, 128:256] = turns[0][3]
    turn_ref[:128, 256:384] = turns[1][0]
    turn_ref[128:, 256:384] = turns[1][2]
    turn_ref[:128, 384:512] = turns[2][1]
    turn_ref[128:, 384:512] = turns[2][3]

    keep.wait()
    keep_z.wait()
    for k in range(raw, 2 * raw + 1):
        forward(k).wait_send()
    for k in range(TILES):
        backward(k).wait()
    for s in range(4):
        whole = recv.at[s, pl.ds(0, ALL - 1)]
        pltpu.make_async_copy(whole, whole, a2a_send).wait()
    for t in range(2):
        whole = arrived.at[t, pl.ds(0, ROWS - 1)]
        pltpu.make_async_copy(whole, whole, rs_send.at[t]).wait()
        whole = flat.at[0, pl.ds(0, 8 * (ROWS - 1))]
        pltpu.make_async_copy(whole, whole, ag_send.at[t]).wait()

    @pl.when(jnp.logical_not(owns_first))
    def _():
        for t in range(2):
            whole = flat.at[0, pl.ds(0, 8 * ROWS)]
            pltpu.make_async_copy(whole, whole, lend_send.at[t]).wait()


def two_steps(v, order, pairing):
    dma = pltpu.SemaphoreType.DMA
    return pl.pallas_call(
        steps_kernel,
        out_shape=(
            jax.ShapeDtypeStruct((4, PIX, 128), F32),
            jax.ShapeDtypeStruct((PIX, 128), F32),
            jax.ShapeDtypeStruct((PIX, 128), F32),
            jax.ShapeDtypeStruct((256, 512), F32),
        ),
        in_specs=[ANY, SMEM, SMEM],
        out_specs=(ANY, ANY, ANY, pl.BlockSpec(memory_space=pltpu.VMEM)),
        scratch_shapes=[
            pltpu.VMEM((8192, 128), F32),
            pltpu.VMEM((8, 2, ROWS, 16, 128), F32),
            pltpu.VMEM((4, ALL, 16, 128), F32),
            pltpu.VMEM((4, PIX, 128), F32),
            pltpu.VMEM((4, PIX, 128), F32),
            pltpu.VMEM((4, PIX, 128), F32),
            pltpu.VMEM((PIX, 128), F32),
            pltpu.VMEM((PIX, 128), F32),
            pltpu.VMEM((PIX, 128), F32),
            pltpu.VMEM((PIX, 128), F32),
            pltpu.VMEM((4, 128), F32),
            pltpu.VMEM((2, ROWS, 10, 128), F32),
            pltpu.VMEM((2, ROWS, 10, 128), F32),
            pltpu.VMEM((2, 8, 128), F32),
            pltpu.VMEM((2, 2, 16, 8, 128), F32),
            pltpu.VMEM((2, 16, 8, 128), F32),
            pltpu.VMEM((3, 256, 256), F32),
            pltpu.VMEM((6, 256, 128), F32),
            pltpu.VMEM((6, 128, 128), F32),
            dma((8,)), dma((2,)), dma, dma((4,)), dma((2,)), dma((2,)), dma((2,)), dma((4,)), dma((2,)), dma((2,)),
            dma((2 * TILES - 1,)), dma((2 * TILES - 1,)), dma((TILES,)), dma((TILES,)),
        ],
        compiler_params=pltpu.CompilerParams(
            collective_id=0, has_side_effects=True, vmem_limit_bytes=VMEM
        ),
    )(v, order, pairing)


def finish_kernel(y_ref, z_ref, qn_ref, turn_ref, pairing_ref, out_ref):
    yc = lax.axis_index("cols")
    a, b, c = roles(pairing_ref[0, yc])
    slots = roles(pairing_ref[1, yc])
    a2, b2, c2 = (jnp.where(slot == a, 0, jnp.where(slot == b, 1, 2)) for slot in slots)
    at = [pl.ds(pl.multiple_of(slot * 128, 128), 128) for slot in slots]
    here = tile(pl.program_id(0))

    def turned(first, second, columns):
        return product(jnp.concatenate([first[here, :], second[here, :]], axis=1), turn_ref[:, columns])

    pair = turned(y_ref.at[a2], y_ref.at[b2], pl.ds(0, 256))
    out_ref[:, at[0]] = pair[:, :128]
    out_ref[:, at[1]] = pair[:, 128:]
    out_ref[:, at[2]] = turned(y_ref.at[c2], z_ref, pl.ds(256, 128))
    out_ref[:, 384:512] = turned(qn_ref, y_ref.at[3], pl.ds(384, 128))


def finish(y, z, qn, turn, pairing):
    rows = TILE
    return pl.pallas_call(
        finish_kernel,
        grid=(PIX // rows,),
        out_shape=jax.ShapeDtypeStruct((PIX, 512), F32),
        in_specs=[INNER, INNER, INNER, INNER, SMEM],
        out_specs=pl.BlockSpec((rows, 512), lambda i: (i, 0)),
        compiler_params=pltpu.CompilerParams(vmem_limit_bytes=24 * 2**20),
    )(y, z, qn, turn, pairing)


def body(tracks, pixel_order, pairing):
    v = tracks.reshape(8, 2, 512, 128).transpose(0, 2, 1, 3).reshape(8192, 128)
    return finish(*two_steps(v, pixel_order, pairing), pairing)


def solution(mesh):
    placed = (P(("rows", "cols"), None, None), P("rows"), P())
    return jax.shard_map(
        body, mesh=mesh, in_specs=placed, out_specs=P("rows", "cols"), check_vma=False
    )
```

```python
import jax
import jax.numpy as jnp
from jax import lax
from jax.experimental import pallas as pl
from jax.experimental.pallas import tpu as pltpu
from jax.sharding import PartitionSpec as P

F32 = jnp.float32
MESH = pl.DeviceIdType.MESH
ANY = pl.BlockSpec(memory_space=pl.ANY)
SMEM = pl.BlockSpec(memory_space=pltpu.SMEM)
INNER = pl.BlockSpec(memory_space=pltpu.VMEM)
HIGH = lax.Precision.HIGH
NS_STEPS = 6
ROWS = 32
COLS = 4
ALL = ROWS * COLS
PIX = 2048
TILE = 512
TILES = PIX // TILE
VMEM = 46 * 2**20


def product(a, b):
    return jnp.dot(a, b, precision=HIGH, preferred_element_type=F32)


def product_of_rows(a, b):
    return lax.dot_general(a, b, (((0,), (0,)), ((), ())), precision=HIGH, preferred_element_type=F32)


def any_peer(i, yr, yc):
    first, second, third = (i >> 1) & 3, (i >> 3) & 3, i >> 5
    y = ((yr >> 3) + first + second) & 3
    x = (((yr >> 1) & 2) + (yc >> 1) + first) & 3
    z = (yr + first + third + 2 * second) & 3
    return (y << 3) + ((x >> 1) << 2) + z, ((x & 1) << 1) + ((yc + i) & 1)


def distance(i):
    first, second, third = i >> 1 & 3, i >> 3 & 3, i >> 5
    return sum((0, 1, 2, 1)[k & 3] for k in (first + second, first, first + third + 2 * second))


def row_peer(i, yr):
    y = ((yr >> 3) + (i >> 2)) & 3
    x = ((yr >> 2) + (i >> 4)) & 1
    z = (yr + i) & 3
    return (y << 3) + (x << 2) + z


def hops(i):
    ring = (0, 1, 2, 1)
    return ring[i & 3] + ring[i >> 2 & 3] + 2 * (i >> 4)


FAR_FIRST = sorted(range(ROWS), key=hops, reverse=True)


def roles(choice):
    low = jnp.where(choice == 2, 1, 0)
    high = jnp.where(choice == 0, 1, 2)
    return low, high, 2 - choice


def tile(i):
    if isinstance(i, int):
        return pl.ds(i * TILE, TILE)
    return pl.ds(pl.multiple_of(i * TILE, TILE), TILE)


def exact(a, b):
    return jnp.dot(a, b, precision=lax.Precision.HIGHEST, preferred_element_type=F32)


def rotations(couplings, state, weight):
    size = 128
    row = lax.broadcasted_iota(jnp.int32, (size, size), 0)
    col = lax.broadcasted_iota(jnp.int32, (size, size), 1)
    eye = jnp.where(row == col, 1.0, 0.0).astype(F32)
    count = 2 * len(couplings)
    flipped = [c.T for c in couplings]
    for k, c in enumerate(couplings):
        total = 1.0 + jnp.sum(jnp.sum(c * c, axis=1, keepdims=True), axis=0, keepdims=True)
        start = eye * (1.0 / jnp.sqrt(total))
        for m, square in ((2 * k, exact(c, flipped[k])), (2 * k + 1, exact(flipped[k], c))):
            weight[m] = eye + square
            state[m, :size, :] = (eye + square) / total
            state[m, size:, :] = start

    def step(_, carry):
        held = [state[m] for m in range(count)]
        factors = [1.5 * eye - 0.5 * h[:size] for h in held]
        once = [product(h, f) for h, f in zip(held, factors)]
        twice = [product(o[:size], f) for o, f in zip(once, factors)]
        for m in range(count):
            state[m, :size, :] = twice[m]
            state[m, size:, :] = once[m][size:]
        return carry

    lax.fori_loop(0, NS_STEPS - 1, step, 0, unroll=True)
    half = [state[m, size:, :] for m in range(count)]
    met = [exact(weight[m], half[m]) for m in range(count)]
    inner = [exact(half[m], met[m]) for m in range(count)]
    crossed = [exact(half[2 * k], c) for k, c in enumerate(couplings)]
    factors = [1.5 * eye - 0.5 * n for n in inner]
    last = [exact(h, f) for h, f in zip(half, factors)]
    out = []
    for k in range(len(couplings)):
        cross = exact(factors[2 * k], crossed[k])
        out.append((last[2 * k], cross, -cross.T, last[2 * k + 1]))
    return out


def steps_kernel(
    v_ref, order_ref, pairing_ref, y_ref, z_ref, qn_ref, turn_ref,
    vv, send, recv, flat, xt, yy, zc, z3, z, q, diag, parts, arrived, own, coup, coupn, rot, state, weight,
    load_sem, out_sem, a2a_send, a2a_recv, rs_send, rs_recv, ag_send, ag_recv, lend_send, lend_recv,
    z_send, z_recv, q_send, q_recv,
):
    yr, yc = lax.axis_index("rows"), lax.axis_index("cols")
    me = yr * COLS + yc
    after, before = (yc + 1) & 3, (yc + 3) & 3
    barrier = pltpu.get_barrier_semaphore()

    def load(frame):
        lines = pl.ds(frame * 1024, 1024)
        return pltpu.make_async_copy(v_ref.at[lines], vv.at[lines], load_sem.at[frame])

    for s in range(4):
        load(s).start()
        load(4 + s).start()

    for i in sorted(range(1, ALL), key=distance, reverse=True):
        pl.semaphore_signal(barrier, inc=1, device_id=any_peer(i, yr, yc), device_id_type=MESH)
    for s in range(4):
        load(s).wait()
        load(4 + s).wait()

        def split(block, carry, s=s):
            for frame in (s, 4 + s):
                for part in range(2):
                    send[frame, part, block] = vv[pl.ds(frame * 1024 + block * 32 + part, 16, stride=2), :]
            return carry

        lax.fori_loop(0, ROWS, split, 0, unroll=2)
        if s == 0:
            pl.semaphore_wait(barrier, ALL - 1)

        def scatter(i, carry, s=s):
            r, c = any_peer(i, yr, yc)
            pltpu.make_async_remote_copy(
                src_ref=send.at[((c & 1) << 2) + s, c >> 1, r], dst_ref=recv.at[s, me],
                send_sem=a2a_send, recv_sem=a2a_recv.at[s],
                device_id=(r, c), device_id_type=MESH,
            ).start()
            return carry

        lax.fori_loop(1, ALL, scatter, 0)
        recv[s, me] = send[((yc & 1) << 2) + s, yc >> 1, yr]

    def gram(left, right):
        def add(i, carry):
            return carry + product_of_rows(left(i), right(i))

        return lax.fori_loop(0, TILES, add, jnp.zeros((128, 128), F32), unroll=True)

    def squares(block):
        def add(i, carry):
            x = block(i)
            return carry + jnp.sum(x * x, axis=0, keepdims=True)

        return lax.fori_loop(0, TILES, add, jnp.zeros((1, 128), F32))

    def place(s):
        def move(i, carry):
            for u in range(16):
                k = i * 16 + u
                xt[s, pl.ds(k, 1), :] = flat[s, pl.ds(order_ref[k] & (PIX - 1), 1), :]
            return carry

        lax.fori_loop(0, PIX // 16, move, 0)

    owns_first = (yr & 1) == 0

    def deal(t, p, cross, diagonals):
        low = jnp.concatenate(diagonals, axis=0)
        for k in range(16):
            parts[t, 2 * k + p, 0:8, :] = cross[8 * k : 8 * k + 8]
            parts[t, 2 * k + p, 8:10, :] = low
        odd = (yr + p) & 1

        def give(m):
            r = row_peer(2 * m + odd, yr)
            pltpu.make_async_remote_copy(
                src_ref=parts.at[t, r], dst_ref=arrived.at[t, yr],
                send_sem=rs_send.at[t], recv_sem=rs_recv.at[t],
                device_id=(r, yc), device_id_type=MESH,
            ).start()

        for m in sorted(range(1, 16), key=lambda m: hops(2 * m + 1), reverse=True):
            give(m)

        @pl.when(odd == 1)
        def _():
            give(0)

        @pl.when(odd == 0)
        def _():
            arrived[t, yr] = parts[t, yr]

    def own_part(t, p):
        whole = arrived.at[t, pl.ds(0, ROWS - 1)]
        pltpu.make_async_copy(whole, whole, rs_recv.at[t]).wait()
        total = arrived[t, 0]
        for r in range(1, ROWS):
            total = total + arrived[t, r]
        left, right = total[8:9], total[9:10]
        spot = lax.broadcasted_iota(jnp.int32, (8, 128), 0) + 8 * (yr >> 1)
        lane = lax.broadcasted_iota(jnp.int32, (8, 128), 1)
        left = jnp.sum(jnp.where(spot == lane, jnp.broadcast_to(left, (8, 128)), 0.0), axis=1, keepdims=True)
        mine = total[0:8] / (left + right)
        own[t] = mine
        coup[t, p, yr >> 1] = mine
        for i in FAR_FIRST[:-1]:
            pltpu.make_async_remote_copy(
                src_ref=own.at[t], dst_ref=coup.at[t, p, yr >> 1],
                send_sem=ag_send.at[t], recv_sem=ag_recv.at[2 * t + p],
                device_id=(row_peer(i, yr), yc), device_id_type=MESH,
            ).start()
        if p == 1:
            for i in FAR_FIRST:
                pltpu.make_async_remote_copy(
                    src_ref=own.at[t], dst_ref=coupn.at[t, yr >> 1],
                    send_sem=lend_send.at[t], recv_sem=lend_recv.at[t],
                    device_id=(row_peer(i, yr), before if t else after), device_id_type=MESH,
                ).start()

    def shared(t, p):
        mine = (yr & 1) == p
        for count, chosen in ((15, mine), (16, jnp.logical_not(mine))):
            @pl.when(chosen)
            def _(count=count):
                whole = coup.at[t, p, pl.ds(0, count)]
                pltpu.make_async_copy(whole, whole, ag_recv.at[2 * t + p]).wait()

        return coup[t, p].reshape(128, 128)

    def lent(t):
        whole = coupn.at[t]
        pltpu.make_async_copy(whole, whole, lend_recv.at[t]).wait()
        return coupn[t].reshape(128, 128)

    raw = TILES - 1

    def forward(k):
        at = pl.ds(k % raw * TILE, TILE)
        pairs = ((q.at[at], zc.at[at]), (xt.at[3, at], z3.at[at]))
        src, dst = pairs[k // raw] if k < 2 * raw else (yy.at[3, pl.ds(raw * TILE, TILE)], z.at[pl.ds(raw * TILE, TILE)])
        return pltpu.make_async_remote_copy(
            src_ref=src, dst_ref=dst, send_sem=z_send.at[k], recv_sem=z_recv.at[k],
            device_id=(yr, after), device_id_type=MESH,
        )

    def square(x):
        return jnp.sum(x * x, axis=0, keepdims=True)

    a, b, c = roles(pairing_ref[0, yc])
    for s in range(4):
        if s == 3:
            gram_p = gram(lambda i: flat[a, tile(i), :], lambda i: flat[b, tile(i), :])
            deal(0, 0, gram_p, (diag[pl.ds(a, 1), :], diag[pl.ds(b, 1), :]))
        whole = recv.at[s, pl.ds(0, ALL - 1)]
        pltpu.make_async_copy(whole, whole, a2a_recv.at[s]).wait()
        if s < 3:
            for g in range(16):
                flat[s, pl.ds(g * 128, 128), :] = recv[s, :, g, :].T
            diag[pl.ds(s, 1), :] = squares(lambda i, s=s: flat[s, tile(i), :])
            place(s)

    q[pl.ds(0, TILE), :] = xt[c, pl.ds(0, TILE), :]
    forward(0).start()
    gram_q = jnp.zeros((128, 128), F32)
    square_3 = jnp.zeros((1, 128), F32)
    span = TILE // 128
    for k in range(TILES):
        block = jnp.concatenate([recv[3, :, span * k + g, :].T for g in range(span)], axis=0)
        flat[3, tile(k), :] = block
        gram_q = gram_q + product_of_rows(flat[c, tile(k), :], block)
        square_3 = square_3 + square(block)

    deal(0, 1, gram_q, (diag[pl.ds(c, 1), :], square_3))

    @pl.when(owns_first)
    def _():
        own_part(0, 0)

    for k in range(1, raw):
        q[pl.ds(k * TILE, TILE), :] = xt[c, pl.ds(k * TILE, TILE), :]
        forward(k).start()
    place(3)

    @pl.when(jnp.logical_not(owns_first))
    def _():
        own_part(0, 1)

    for k in range(raw, 2 * raw):
        forward(k).start()

    def keep_rotation(k, parts_of):
        top, cross, down, low = parts_of
        rot[k, :128, :128] = top
        rot[k, :128, 128:] = cross
        rot[k, 128:, :128] = down
        rot[k, 128:, 128:] = low

    def turn_second(i):
        x = jnp.concatenate([xt[c, tile(i), :], xt[3, tile(i), :]], axis=1)
        turned = product(x, rot[1])
        yy[3, tile(i), :] = turned[:, 128:]
        yy[2, tile(i), :] = turned[:, :128]
        return square(turned[:, :128])

    def turn_first(i):
        x = jnp.concatenate([xt[a, tile(i), :], xt[b, tile(i), :]], axis=1)
        turned = product(x, rot[0])
        yy[0, tile(i), :] = turned[:, :128]
        yy[1, tile(i), :] = turned[:, 128:]
        return square(turned)

    keep_rotation(0, rotations((shared(0, 0),), state, weight)[0])
    square_ab = lax.fori_loop(
        0, TILES, lambda i, carry: carry + turn_first(i), jnp.zeros((1, 256), F32), unroll=True
    )
    for k, turn in enumerate(rotations((shared(0, 1), lent(0)), state, weight)):
        keep_rotation(1 + k, turn)
    square_c = turn_second(raw)
    forward(2 * raw).start()
    square_c = lax.fori_loop(0, raw, lambda i, carry: carry + turn_second(i), square_c, unroll=True)
    diag[0:1, :] = square_ab[:, :128]
    diag[1:2, :] = square_ab[:, 128:]
    diag[2:3, :] = square_c
    keep = pltpu.make_async_copy(yy, y_ref, out_sem.at[0])

    def role_of(slot):
        return jnp.where(slot == a, 0, jnp.where(slot == b, 1, 2))

    a2, b2, c2 = (role_of(slot) for slot in roles(pairing_ref[1, yc]))
    gram_p = gram(lambda i: yy[a2, tile(i), :], lambda i: yy[b2, tile(i), :])
    deal(1, 0, gram_p, (diag[pl.ds(a2, 1), :], diag[pl.ds(b2, 1), :]))

    for k in range(2 * raw):
        forward(k).wait_recv()

    def meet(i, block, carry):
        total, norms = carry
        return (
            total + product_of_rows(yy[c2, tile(i), :], block),
            norms + square(block),
        )

    def turn_and_meet(i, carry):
        x = jnp.concatenate([zc[tile(i), :], z3[tile(i), :]], axis=1)
        block = product(x, rot[2, :, 128:])
        z[tile(i), :] = block
        return meet(i, block, carry)

    met = lax.fori_loop(
        0, raw, turn_and_meet, (jnp.zeros((128, 128), F32), jnp.zeros((1, 128), F32)), unroll=True
    )
    forward(2 * raw).wait_recv()
    gram_q, last = meet(raw, z[tile(raw), :], met)
    keep_z = pltpu.make_async_copy(z, z_ref, out_sem.at[1])
    for k in range(raw):
        forward(k).wait_send()

    def backward(k):
        part = tile(k)
        return pltpu.make_async_remote_copy(
            src_ref=q.at[part], dst_ref=qn_ref.at[part], send_sem=q_send.at[k], recv_sem=q_recv.at[k],
            device_id=(yr, before), device_id_type=MESH,
        )

    deal(1, 1, gram_q, (diag[pl.ds(c2, 1), :], last))
    for k in range(TILES):
        q[tile(k), :] = yy[c2, tile(k), :]
    backward(0).start()

    @pl.when(owns_first)
    def _():
        own_part(1, 0)
        backward(1).start()

    @pl.when(jnp.logical_not(owns_first))
    def _():
        backward(1).start()
        own_part(1, 1)

    for k in range(2, TILES):
        backward(k).start()
    keep.start()
    keep_z.start()
    turns = rotations((shared(1, 0),), state, weight)
    turns += rotations((shared(1, 1), lent(1)), state, weight)
    turn_ref[:128, 0:128] = turns[0][0]
    turn_ref[:128, 128:256] = turns[0][1]
    turn_ref[128:, 0:128] = turns[0][2]
    turn_ref[128:, 128:256] = turns[0][3]
    turn_ref[:128, 256:384] = turns[1][0]
    turn_ref[128:, 256:384] = turns[1][2]
    turn_ref[:128, 384:512] = turns[2][1]
    turn_ref[128:, 384:512] = turns[2][3]

    keep.wait()
    keep_z.wait()
    for k in range(raw, 2 * raw + 1):
        forward(k).wait_send()
    for k in range(TILES):
        backward(k).wait()
    for s in range(4):
        whole = recv.at[s, pl.ds(0, ALL - 1)]
        pltpu.make_async_copy(whole, whole, a2a_send).wait()
    for t in range(2):
        whole = arrived.at[t, pl.ds(0, ROWS - 1)]
        pltpu.make_async_copy(whole, whole, rs_send.at[t]).wait()
        whole = flat.at[0, pl.ds(0, 8 * (ROWS - 1))]
        pltpu.make_async_copy(whole, whole, ag_send.at[t]).wait()

    @pl.when(jnp.logical_not(owns_first))
    def _():
        for t in range(2):
            whole = flat.at[0, pl.ds(0, 8 * ROWS)]
            pltpu.make_async_copy(whole, whole, lend_send.at[t]).wait()


def two_steps(v, order, pairing):
    dma = pltpu.SemaphoreType.DMA
    return pl.pallas_call(
        steps_kernel,
        out_shape=(
            jax.ShapeDtypeStruct((4, PIX, 128), F32),
            jax.ShapeDtypeStruct((PIX, 128), F32),
            jax.ShapeDtypeStruct((PIX, 128), F32),
            jax.ShapeDtypeStruct((256, 512), F32),
        ),
        in_specs=[ANY, SMEM, SMEM],
        out_specs=(ANY, ANY, ANY, pl.BlockSpec(memory_space=pltpu.VMEM)),
        scratch_shapes=[
            pltpu.VMEM((8192, 128), F32),
            pltpu.VMEM((8, 2, ROWS, 16, 128), F32),
            pltpu.VMEM((4, ALL, 16, 128), F32),
            pltpu.VMEM((4, PIX, 128), F32),
            pltpu.VMEM((4, PIX, 128), F32),
            pltpu.VMEM((4, PIX, 128), F32),
            pltpu.VMEM((PIX, 128), F32),
            pltpu.VMEM((PIX, 128), F32),
            pltpu.VMEM((PIX, 128), F32),
            pltpu.VMEM((PIX, 128), F32),
            pltpu.VMEM((4, 128), F32),
            pltpu.VMEM((2, ROWS, 10, 128), F32),
            pltpu.VMEM((2, ROWS, 10, 128), F32),
            pltpu.VMEM((2, 8, 128), F32),
            pltpu.VMEM((2, 2, 16, 8, 128), F32),
            pltpu.VMEM((2, 16, 8, 128), F32),
            pltpu.VMEM((3, 256, 256), F32),
            pltpu.VMEM((6, 256, 128), F32),
            pltpu.VMEM((6, 128, 128), F32),
            dma((8,)), dma((2,)), dma, dma((4,)), dma((2,)), dma((2,)), dma((2,)), dma((4,)), dma((2,)), dma((2,)),
            dma((2 * TILES - 1,)), dma((2 * TILES - 1,)), dma((TILES,)), dma((TILES,)),
        ],
        compiler_params=pltpu.CompilerParams(
            collective_id=0, has_side_effects=True, vmem_limit_bytes=VMEM
        ),
    )(v, order, pairing)


def finish_kernel(y_ref, z_ref, qn_ref, turn_ref, pairing_ref, out_ref):
    yc = lax.axis_index("cols")
    a, b, c = roles(pairing_ref[0, yc])
    slots = roles(pairing_ref[1, yc])
    a2, b2, c2 = (jnp.where(slot == a, 0, jnp.where(slot == b, 1, 2)) for slot in slots)
    at = [pl.ds(pl.multiple_of(slot * 128, 128), 128) for slot in slots]
    here = tile(pl.program_id(0))

    def turned(first, second, columns):
        return product(jnp.concatenate([first[here, :], second[here, :]], axis=1), turn_ref[:, columns])

    pair = turned(y_ref.at[a2], y_ref.at[b2], pl.ds(0, 256))
    out_ref[:, at[0]] = pair[:, :128]
    out_ref[:, at[1]] = pair[:, 128:]
    out_ref[:, at[2]] = turned(y_ref.at[c2], z_ref, pl.ds(256, 128))
    out_ref[:, 384:512] = turned(qn_ref, y_ref.at[3], pl.ds(384, 128))


def finish(y, z, qn, turn, pairing):
    rows = TILE
    return pl.pallas_call(
        finish_kernel,
        grid=(PIX // rows,),
        out_shape=jax.ShapeDtypeStruct((PIX, 512), F32),
        in_specs=[INNER, INNER, INNER, INNER, SMEM],
        out_specs=pl.BlockSpec((rows, 512), lambda i: (i, 0)),
        compiler_params=pltpu.CompilerParams(vmem_limit_bytes=24 * 2**20),
    )(y, z, qn, turn, pairing)


def body(tracks, pixel_order, pairing):
    v = tracks.reshape(8, 2, 512, 128).transpose(0, 2, 1, 3).reshape(8192, 128)
    return finish(*two_steps(v, pixel_order, pairing), pairing)


def solution(mesh):
    placed = (P(("rows", "cols"), None, None), P("rows"), P())
    return jax.shard_map(
        body, mesh=mesh, in_specs=placed, out_specs=P("rows", "cols"), check_vma=False
    )
```

```python
import jax
import jax.numpy as jnp
from jax import lax
from jax.experimental import pallas as pl
from jax.experimental.pallas import tpu as pltpu
from jax.sharding import PartitionSpec as P

F32 = jnp.float32
MESH = pl.DeviceIdType.MESH
ANY = pl.BlockSpec(memory_space=pl.ANY)
SMEM = pl.BlockSpec(memory_space=pltpu.SMEM)
INNER = pl.BlockSpec(memory_space=pltpu.VMEM)
HIGH = lax.Precision.HIGH
NS_STEPS = 6
ROWS = 32
COLS = 4
ALL = ROWS * COLS
PIX = 2048
TILE = 512
TILES = PIX // TILE
VMEM = 46 * 2**20


def product(a, b):
    return jnp.dot(a, b, precision=HIGH, preferred_element_type=F32)


def product_of_rows(a, b):
    return lax.dot_general(a, b, (((0,), (0,)), ((), ())), precision=HIGH, preferred_element_type=F32)


def any_peer(i, yr, yc):
    first, second, third = (i >> 1) & 3, (i >> 3) & 3, i >> 5
    y = ((yr >> 3) + first + second) & 3
    x = (((yr >> 1) & 2) + (yc >> 1) + first) & 3
    z = (yr + first + third + 2 * second) & 3
    return (y << 3) + ((x >> 1) << 2) + z, ((x & 1) << 1) + ((yc + i) & 1)


def distance(i):
    first, second, third = i >> 1 & 3, i >> 3 & 3, i >> 5
    return sum((0, 1, 2, 1)[k & 3] for k in (first + second, first, first + third + 2 * second))


def row_peer(i, yr):
    y = ((yr >> 3) + (i >> 2)) & 3
    x = ((yr >> 2) + (i >> 4)) & 1
    z = (yr + i) & 3
    return (y << 3) + (x << 2) + z


def hops(i):
    ring = (0, 1, 2, 1)
    return ring[i & 3] + ring[i >> 2 & 3] + 2 * (i >> 4)


FAR_FIRST = sorted(range(ROWS), key=hops, reverse=True)


def roles(choice):
    low = jnp.where(choice == 2, 1, 0)
    high = jnp.where(choice == 0, 1, 2)
    return low, high, 2 - choice


def tile(i):
    if isinstance(i, int):
        return pl.ds(i * TILE, TILE)
    return pl.ds(pl.multiple_of(i * TILE, TILE), TILE)


def exact(a, b):
    return jnp.dot(a, b, precision=lax.Precision.HIGHEST, preferred_element_type=F32)


def rotations(couplings, state, weight):
    size = 128
    row = lax.broadcasted_iota(jnp.int32, (size, size), 0)
    col = lax.broadcasted_iota(jnp.int32, (size, size), 1)
    eye = jnp.where(row == col, 1.0, 0.0).astype(F32)
    count = 2 * len(couplings)
    flipped = [c.T for c in couplings]
    for k, c in enumerate(couplings):
        total = 1.0 + jnp.sum(jnp.sum(c * c, axis=1, keepdims=True), axis=0, keepdims=True)
        start = eye * (1.0 / jnp.sqrt(total))
        for m, square in ((2 * k, exact(c, flipped[k])), (2 * k + 1, exact(flipped[k], c))):
            weight[m] = eye + square
            state[m, :size, :] = (eye + square) / total
            state[m, size:, :] = start

    def step(_, carry):
        held = [state[m] for m in range(count)]
        factors = [1.5 * eye - 0.5 * h[:size] for h in held]
        once = [product(h, f) for h, f in zip(held, factors)]
        twice = [product(o[:size], f) for o, f in zip(once, factors)]
        for m in range(count):
            state[m, :size, :] = twice[m]
            state[m, size:, :] = once[m][size:]
        return carry

    lax.fori_loop(0, NS_STEPS - 1, step, 0, unroll=True)
    half = [state[m, size:, :] for m in range(count)]
    met = [exact(weight[m], half[m]) for m in range(count)]
    inner = [exact(half[m], met[m]) for m in range(count)]
    crossed = [exact(half[2 * k], c) for k, c in enumerate(couplings)]
    factors = [1.5 * eye - 0.5 * n for n in inner]
    last = [exact(h, f) for h, f in zip(half, factors)]
    out = []
    for k in range(len(couplings)):
        cross = exact(factors[2 * k], crossed[k])
        out.append((last[2 * k], cross, -cross.T, last[2 * k + 1]))
    return out


def steps_kernel(
    v_ref, order_ref, pairing_ref, y_ref, z_ref, qn_ref, turn_ref,
    vv, send, recv, flat, xt, yy, zc, z3, z, q, diag, parts, arrived, own, coup, coupn, rot, state, weight,
    load_sem, out_sem, a2a_send, a2a_recv, rs_send, rs_recv, ag_send, ag_recv, lend_send, lend_recv,
    z_send, z_recv, q_send, q_recv,
):
    yr, yc = lax.axis_index("rows"), lax.axis_index("cols")
    me = yr * COLS + yc
    after, before = (yc + 1) & 3, (yc + 3) & 3
    barrier = pltpu.get_barrier_semaphore()

    def load(frame):
        lines = pl.ds(frame * 1024, 1024)
        return pltpu.make_async_copy(v_ref.at[lines], vv.at[lines], load_sem.at[frame])

    for s in range(4):
        load(s).start()
        load(4 + s).start()

    for i in sorted(range(1, ALL), key=distance, reverse=True):
        pl.semaphore_signal(barrier, inc=1, device_id=any_peer(i, yr, yc), device_id_type=MESH)
    for s in range(4):
        load(s).wait()
        load(4 + s).wait()

        def split(block, carry, s=s):
            for frame in (s, 4 + s):
                for part in range(2):
                    send[frame, part, block] = vv[pl.ds(frame * 1024 + block * 32 + part, 16, stride=2), :]
            return carry

        lax.fori_loop(0, ROWS, split, 0, unroll=2)
        if s == 0:
            pl.semaphore_wait(barrier, ALL - 1)

        def scatter(i, carry, s=s):
            r, c = any_peer(i, yr, yc)
            pltpu.make_async_remote_copy(
                src_ref=send.at[((c & 1) << 2) + s, c >> 1, r], dst_ref=recv.at[s, me],
                send_sem=a2a_send, recv_sem=a2a_recv.at[s],
                device_id=(r, c), device_id_type=MESH,
            ).start()
            return carry

        lax.fori_loop(1, ALL, scatter, 0, unroll=4)
        recv[s, me] = send[((yc & 1) << 2) + s, yc >> 1, yr]

    def gram(left, right):
        def add(i, carry):
            return carry + product_of_rows(left(i), right(i))

        return lax.fori_loop(0, TILES, add, jnp.zeros((128, 128), F32), unroll=True)

    def squares(block):
        def add(i, carry):
            x = block(i)
            return carry + jnp.sum(x * x, axis=0, keepdims=True)

        return lax.fori_loop(0, TILES, add, jnp.zeros((1, 128), F32))

    def place(s):
        def move(i, carry):
            for u in range(16):
                k = i * 16 + u
                xt[s, pl.ds(k, 1), :] = flat[s, pl.ds(order_ref[k] & (PIX - 1), 1), :]
            return carry

        lax.fori_loop(0, PIX // 16, move, 0)

    owns_first = (yr & 1) == 0

    def deal(t, p, cross, diagonals):
        low = jnp.concatenate(diagonals, axis=0)
        for k in range(16):
            parts[t, 2 * k + p, 0:8, :] = cross[8 * k : 8 * k + 8]
            parts[t, 2 * k + p, 8:10, :] = low
        odd = (yr + p) & 1

        def give(m):
            r = row_peer(2 * m + odd, yr)
            pltpu.make_async_remote_copy(
                src_ref=parts.at[t, r], dst_ref=arrived.at[t, yr],
                send_sem=rs_send.at[t], recv_sem=rs_recv.at[t],
                device_id=(r, yc), device_id_type=MESH,
            ).start()

        for m in sorted(range(1, 16), key=lambda m: hops(2 * m + 1), reverse=True):
            give(m)

        @pl.when(odd == 1)
        def _():
            give(0)

        @pl.when(odd == 0)
        def _():
            arrived[t, yr] = parts[t, yr]

    def own_part(t, p):
        whole = arrived.at[t, pl.ds(0, ROWS - 1)]
        pltpu.make_async_copy(whole, whole, rs_recv.at[t]).wait()
        total = arrived[t, 0]
        for r in range(1, ROWS):
            total = total + arrived[t, r]
        left, right = total[8:9], total[9:10]
        spot = lax.broadcasted_iota(jnp.int32, (8, 128), 0) + 8 * (yr >> 1)
        lane = lax.broadcasted_iota(jnp.int32, (8, 128), 1)
        left = jnp.sum(jnp.where(spot == lane, jnp.broadcast_to(left, (8, 128)), 0.0), axis=1, keepdims=True)
        mine = total[0:8] / (left + right)
        own[t] = mine
        coup[t, p, yr >> 1] = mine
        for i in FAR_FIRST[:-1]:
            pltpu.make_async_remote_copy(
                src_ref=own.at[t], dst_ref=coup.at[t, p, yr >> 1],
                send_sem=ag_send.at[t], recv_sem=ag_recv.at[2 * t + p],
                device_id=(row_peer(i, yr), yc), device_id_type=MESH,
            ).start()
        if p == 1:
            for i in FAR_FIRST:
                pltpu.make_async_remote_copy(
                    src_ref=own.at[t], dst_ref=coupn.at[t, yr >> 1],
                    send_sem=lend_send.at[t], recv_sem=lend_recv.at[t],
                    device_id=(row_peer(i, yr), before if t else after), device_id_type=MESH,
                ).start()

    def shared(t, p):
        mine = (yr & 1) == p
        for count, chosen in ((15, mine), (16, jnp.logical_not(mine))):
            @pl.when(chosen)
            def _(count=count):
                whole = coup.at[t, p, pl.ds(0, count)]
                pltpu.make_async_copy(whole, whole, ag_recv.at[2 * t + p]).wait()

        return coup[t, p].reshape(128, 128)

    def lent(t):
        whole = coupn.at[t]
        pltpu.make_async_copy(whole, whole, lend_recv.at[t]).wait()
        return coupn[t].reshape(128, 128)

    raw = TILES - 1

    def forward(k):
        at = pl.ds(k % raw * TILE, TILE)
        pairs = ((q.at[at], zc.at[at]), (xt.at[3, at], z3.at[at]))
        src, dst = pairs[k // raw] if k < 2 * raw else (yy.at[3, pl.ds(raw * TILE, TILE)], z.at[pl.ds(raw * TILE, TILE)])
        return pltpu.make_async_remote_copy(
            src_ref=src, dst_ref=dst, send_sem=z_send.at[k], recv_sem=z_recv.at[k],
            device_id=(yr, after), device_id_type=MESH,
        )

    def square(x):
        return jnp.sum(x * x, axis=0, keepdims=True)

    a, b, c = roles(pairing_ref[0, yc])
    for s in range(4):
        if s == 3:
            gram_p = gram(lambda i: flat[a, tile(i), :], lambda i: flat[b, tile(i), :])
            deal(0, 0, gram_p, (diag[pl.ds(a, 1), :], diag[pl.ds(b, 1), :]))
        whole = recv.at[s, pl.ds(0, ALL - 1)]
        pltpu.make_async_copy(whole, whole, a2a_recv.at[s]).wait()
        if s < 3:
            for g in range(16):
                flat[s, pl.ds(g * 128, 128), :] = recv[s, :, g, :].T
            diag[pl.ds(s, 1), :] = squares(lambda i, s=s: flat[s, tile(i), :])
            place(s)

    q[pl.ds(0, TILE), :] = xt[c, pl.ds(0, TILE), :]
    forward(0).start()
    gram_q = jnp.zeros((128, 128), F32)
    square_3 = jnp.zeros((1, 128), F32)
    span = TILE // 128
    for k in range(TILES):
        block = jnp.concatenate([recv[3, :, span * k + g, :].T for g in range(span)], axis=0)
        flat[3, tile(k), :] = block
        gram_q = gram_q + product_of_rows(flat[c, tile(k), :], block)
        square_3 = square_3 + square(block)

    deal(0, 1, gram_q, (diag[pl.ds(c, 1), :], square_3))

    @pl.when(owns_first)
    def _():
        own_part(0, 0)

    for k in range(1, raw):
        q[pl.ds(k * TILE, TILE), :] = xt[c, pl.ds(k * TILE, TILE), :]
        forward(k).start()
    place(3)

    @pl.when(jnp.logical_not(owns_first))
    def _():
        own_part(0, 1)

    for k in range(raw, 2 * raw):
        forward(k).start()

    def keep_rotation(k, parts_of):
        top, cross, down, low = parts_of
        rot[k, :128, :128] = top
        rot[k, :128, 128:] = cross
        rot[k, 128:, :128] = down
        rot[k, 128:, 128:] = low

    def turn_second(i):
        x = jnp.concatenate([xt[c, tile(i), :], xt[3, tile(i), :]], axis=1)
        turned = product(x, rot[1])
        yy[3, tile(i), :] = turned[:, 128:]
        yy[2, tile(i), :] = turned[:, :128]
        return square(turned[:, :128])

    def turn_first(i):
        x = jnp.concatenate([xt[a, tile(i), :], xt[b, tile(i), :]], axis=1)
        turned = product(x, rot[0])
        yy[0, tile(i), :] = turned[:, :128]
        yy[1, tile(i), :] = turned[:, 128:]
        return square(turned)

    keep_rotation(0, rotations((shared(0, 0),), state, weight)[0])
    square_ab = lax.fori_loop(
        0, TILES, lambda i, carry: carry + turn_first(i), jnp.zeros((1, 256), F32), unroll=True
    )
    for k, turn in enumerate(rotations((shared(0, 1), lent(0)), state, weight)):
        keep_rotation(1 + k, turn)
    square_c = turn_second(raw)
    forward(2 * raw).start()
    square_c = lax.fori_loop(0, raw, lambda i, carry: carry + turn_second(i), square_c, unroll=True)
    diag[0:1, :] = square_ab[:, :128]
    diag[1:2, :] = square_ab[:, 128:]
    diag[2:3, :] = square_c
    keep = pltpu.make_async_copy(yy, y_ref, out_sem.at[0])

    def role_of(slot):
        return jnp.where(slot == a, 0, jnp.where(slot == b, 1, 2))

    a2, b2, c2 = (role_of(slot) for slot in roles(pairing_ref[1, yc]))
    gram_p = gram(lambda i: yy[a2, tile(i), :], lambda i: yy[b2, tile(i), :])
    deal(1, 0, gram_p, (diag[pl.ds(a2, 1), :], diag[pl.ds(b2, 1), :]))

    for k in range(2 * raw):
        forward(k).wait_recv()

    def meet(i, block, carry):
        total, norms = carry
        return (
            total + product_of_rows(yy[c2, tile(i), :], block),
            norms + square(block),
        )

    def turn_and_meet(i, carry):
        x = jnp.concatenate([zc[tile(i), :], z3[tile(i), :]], axis=1)
        block = product(x, rot[2, :, 128:])
        z[tile(i), :] = block
        return meet(i, block, carry)

    met = lax.fori_loop(
        0, raw, turn_and_meet, (jnp.zeros((128, 128), F32), jnp.zeros((1, 128), F32)), unroll=True
    )
    forward(2 * raw).wait_recv()
    gram_q, last = meet(raw, z[tile(raw), :], met)
    keep_z = pltpu.make_async_copy(z, z_ref, out_sem.at[1])
    for k in range(raw):
        forward(k).wait_send()

    def backward(k):
        part = tile(k)
        return pltpu.make_async_remote_copy(
            src_ref=q.at[part], dst_ref=qn_ref.at[part], send_sem=q_send.at[k], recv_sem=q_recv.at[k],
            device_id=(yr, before), device_id_type=MESH,
        )

    deal(1, 1, gram_q, (diag[pl.ds(c2, 1), :], last))
    for k in range(TILES):
        q[tile(k), :] = yy[c2, tile(k), :]
    backward(0).start()

    @pl.when(owns_first)
    def _():
        own_part(1, 0)
        backward(1).start()

    @pl.when(jnp.logical_not(owns_first))
    def _():
        backward(1).start()
        own_part(1, 1)

    for k in range(2, TILES):
        backward(k).start()
    keep.start()
    keep_z.start()
    turns = rotations((shared(1, 0),), state, weight)
    turns += rotations((shared(1, 1), lent(1)), state, weight)
    turn_ref[:128, 0:128] = turns[0][0]
    turn_ref[:128, 128:256] = turns[0][1]
    turn_ref[128:, 0:128] = turns[0][2]
    turn_ref[128:, 128:256] = turns[0][3]
    turn_ref[:128, 256:384] = turns[1][0]
    turn_ref[128:, 256:384] = turns[1][2]
    turn_ref[:128, 384:512] = turns[2][1]
    turn_ref[128:, 384:512] = turns[2][3]

    keep.wait()
    keep_z.wait()
    for k in range(raw, 2 * raw + 1):
        forward(k).wait_send()
    for k in range(TILES):
        backward(k).wait()
    for s in range(4):
        whole = recv.at[s, pl.ds(0, ALL - 1)]
        pltpu.make_async_copy(whole, whole, a2a_send).wait()
    for t in range(2):
        whole = arrived.at[t, pl.ds(0, ROWS - 1)]
        pltpu.make_async_copy(whole, whole, rs_send.at[t]).wait()
        whole = flat.at[0, pl.ds(0, 8 * (ROWS - 1))]
        pltpu.make_async_copy(whole, whole, ag_send.at[t]).wait()

    @pl.when(jnp.logical_not(owns_first))
    def _():
        for t in range(2):
            whole = flat.at[0, pl.ds(0, 8 * ROWS)]
            pltpu.make_async_copy(whole, whole, lend_send.at[t]).wait()


def two_steps(v, order, pairing):
    dma = pltpu.SemaphoreType.DMA
    return pl.pallas_call(
        steps_kernel,
        out_shape=(
            jax.ShapeDtypeStruct((4, PIX, 128), F32),
            jax.ShapeDtypeStruct((PIX, 128), F32),
            jax.ShapeDtypeStruct((PIX, 128), F32),
            jax.ShapeDtypeStruct((256, 512), F32),
        ),
        in_specs=[ANY, SMEM, SMEM],
        out_specs=(ANY, ANY, ANY, pl.BlockSpec(memory_space=pltpu.VMEM)),
        scratch_shapes=[
            pltpu.VMEM((8192, 128), F32),
            pltpu.VMEM((8, 2, ROWS, 16, 128), F32),
            pltpu.VMEM((4, ALL, 16, 128), F32),
            pltpu.VMEM((4, PIX, 128), F32),
            pltpu.VMEM((4, PIX, 128), F32),
            pltpu.VMEM((4, PIX, 128), F32),
            pltpu.VMEM((PIX, 128), F32),
            pltpu.VMEM((PIX, 128), F32),
            pltpu.VMEM((PIX, 128), F32),
            pltpu.VMEM((PIX, 128), F32),
            pltpu.VMEM((4, 128), F32),
            pltpu.VMEM((2, ROWS, 10, 128), F32),
            pltpu.VMEM((2, ROWS, 10, 128), F32),
            pltpu.VMEM((2, 8, 128), F32),
            pltpu.VMEM((2, 2, 16, 8, 128), F32),
            pltpu.VMEM((2, 16, 8, 128), F32),
            pltpu.VMEM((3, 256, 256), F32),
            pltpu.VMEM((6, 256, 128), F32),
            pltpu.VMEM((6, 128, 128), F32),
            dma((8,)), dma((2,)), dma, dma((4,)), dma((2,)), dma((2,)), dma((2,)), dma((4,)), dma((2,)), dma((2,)),
            dma((2 * TILES - 1,)), dma((2 * TILES - 1,)), dma((TILES,)), dma((TILES,)),
        ],
        compiler_params=pltpu.CompilerParams(
            collective_id=0, has_side_effects=True, vmem_limit_bytes=VMEM
        ),
    )(v, order, pairing)


def finish_kernel(y_ref, z_ref, qn_ref, turn_ref, pairing_ref, out_ref):
    yc = lax.axis_index("cols")
    a, b, c = roles(pairing_ref[0, yc])
    slots = roles(pairing_ref[1, yc])
    a2, b2, c2 = (jnp.where(slot == a, 0, jnp.where(slot == b, 1, 2)) for slot in slots)
    at = [pl.ds(pl.multiple_of(slot * 128, 128), 128) for slot in slots]
    here = tile(pl.program_id(0))

    def turned(first, second, columns):
        return product(jnp.concatenate([first[here, :], second[here, :]], axis=1), turn_ref[:, columns])

    pair = turned(y_ref.at[a2], y_ref.at[b2], pl.ds(0, 256))
    out_ref[:, at[0]] = pair[:, :128]
    out_ref[:, at[1]] = pair[:, 128:]
    out_ref[:, at[2]] = turned(y_ref.at[c2], z_ref, pl.ds(256, 128))
    out_ref[:, 384:512] = turned(qn_ref, y_ref.at[3], pl.ds(384, 128))


def finish(y, z, qn, turn, pairing):
    rows = TILE
    return pl.pallas_call(
        finish_kernel,
        grid=(PIX // rows,),
        out_shape=jax.ShapeDtypeStruct((PIX, 512), F32),
        in_specs=[INNER, INNER, INNER, INNER, SMEM],
        out_specs=pl.BlockSpec((rows, 512), lambda i: (i, 0)),
        compiler_params=pltpu.CompilerParams(vmem_limit_bytes=24 * 2**20),
    )(y, z, qn, turn, pairing)


def body(tracks, pixel_order, pairing):
    v = tracks.reshape(8, 2, 512, 128).transpose(0, 2, 1, 3).reshape(8192, 128)
    return finish(*two_steps(v, pixel_order, pairing), pairing)


def solution(mesh):
    placed = (P(("rows", "cols"), None, None), P("rows"), P())
    return jax.shard_map(
        body, mesh=mesh, in_specs=placed, out_specs=P("rows", "cols"), check_vma=False
    )
```
